256 devices in a mesh: dp: 2 (over y_lo), ctx: 16 (over y_hi, z), tensor: 8 (over x, core).
Axes of the slice: x: 4, y: 4 (y_hi: 2, y_lo: 2; y = y_hi * 2 + y_lo), z: 8, core: 2. Of those that a mesh axis runs over, the one named last changes fastest.
Arguments:
- input_spikes: int32 [512, 8192], P(None, ('dp', 'ctx')), may hold values from 0 to 65535
- query_spikes: int32 [512, 8192], P('tensor', ('dp', 'ctx')), may hold values from 0 to 65535
- key_spikes: int32 [512, 8192], P('tensor', ('dp', 'ctx')), may hold values from 0 to 65535
- values: bfloat16 [8192, 8192], P(('dp', 'ctx'), 'tensor'), may hold values from -6 to 6
- query_slope: bfloat16 [8192, 8192], P(('dp', 'ctx'), 'tensor'), may hold values from 0.25 to 2
- key_slope: bfloat16 [8192, 8192], P(('dp', 'ctx'), 'tensor'), may hold values from 0.25 to 2
- grad_out: bfloat16 [8192, 8192], P(('dp', 'ctx'), 'tensor'), may hold values from -6 to 6
- log_gate: float32 [64, 8192], P('tensor', ('dp', 'ctx')), may hold values from -0.8 to 0
- pattern: int32 [128, 16], P('tensor'), may hold values from 0 to 127, all different within a row
Outputs:
- query_grad: bfloat16 [8192, 8192], P(('dp', 'ctx'), 'tensor')
- key_grad: bfloat16 [8192, 8192], P(('dp', 'ctx'), 'tensor')
- value_grad: float32 [16, 128, 4096], P('ctx', 'tensor')
The draws below stay inside these ranges and needn't reach their ends.
Inputs may be any that keep to these rules, and one draw needn't show every extreme that they name: `pattern`: each column block names 16 different row blocks.
All inputs are finite; a program needn't handle non-finite values.
Results may differ from the reference program's by a relative error of at most 0.0073.
Values sent between devices are 32-bit elements; how exact they have to be, the bound alone decides.
A program may use at most 128 MiB of HBM per device.

```python
import math
import jax
import jax.numpy as jnp
from jax import lax

D = 8192
ATTENTION_PLANES = 64
HEAD = 128
BLK = 64
TOK_DEV = 256
HE = 8192
NRB = 128
NCB = 128
SEL = 16
SPAN_PER_SERIES = 4096
ALL_ITEMS = 8192


def log_uniform(key, shape, lower_end, upper_end):
    spread = jax.random.uniform(key, shape, jnp.float32)
    return jnp.exp(jnp.log(lower_end) + spread * (jnp.log(upper_end) - jnp.log(lower_end)))


def draw_log_gate(key, part):
    whole_lookup_vectors = jax.random.split(key, 7)
    fast_share = 0.5
    is_fast = jax.random.uniform(whole_lookup_vectors[0], (ATTENTION_PLANES,), jnp.float32) < fast_share
    slow_rate = log_uniform(whole_lookup_vectors[1], (ATTENTION_PLANES,), 0.05, 0.5) / SPAN_PER_SERIES
    fast_rate = log_uniform(whole_lookup_vectors[2], (ATTENTION_PLANES,), 1.0 / 50.0, 1.0 / 30.0)
    head_rate = jnp.where(is_fast, fast_rate, slow_rate)
    block_factor = log_uniform(whole_lookup_vectors[3], (ALL_ITEMS // TOK_DEV,), 0.5, 2.0)
    token_factor = log_uniform(whole_lookup_vectors[4], (ATTENTION_PLANES, ALL_ITEMS), 0.7, 1.4)
    item_indices = jnp.arange(ALL_ITEMS, dtype=jnp.int32)
    block_scale = jnp.take(block_factor, item_indices // TOK_DEV)
    stable_phase_flag = -head_rate[:, None] * block_scale[None, :] * token_factor
    series_number = ALL_ITEMS // SPAN_PER_SERIES
    spike_run_start = jax.random.randint(whole_lookup_vectors[5], (ATTENTION_PLANES, series_number, 2), 0, SPAN_PER_SERIES)
    spike_run_start = spike_run_start + (jnp.arange(series_number, dtype=jnp.int32) * SPAN_PER_SERIES)[None, :, None]
    spike_run_filter = jnp.any(item_indices[None, None, None, :] == spike_run_start[:, :, :, None], axis=(1, 2))
    spike_run_width = jax.random.uniform(whole_lookup_vectors[6], (ATTENTION_PLANES, ALL_ITEMS), jnp.float32, 0.22, 0.69)
    return stable_phase_flag - jnp.where(spike_run_filter, spike_run_width, 0.0)


def plant(entries, stream_key, smallest, largest):
    longest = entries.shape.index(max(entries.shape))
    spots = []
    for shift in (0, 1):
        where = [jax.random.randint(jax.random.fold_in(stream_key, axis), (), 0, length) for axis, length in enumerate(entries.shape)]
        where[longest] = (where[longest] + shift) % entries.shape[longest]
        spots.append(tuple(where))
    return entries.at[spots[0]].set(smallest).at[spots[1]].set(largest)


def level_of(key, dims, cuts, least, top_value):
    def one(axis_at, parts):
        draws = jax.random.uniform(jax.random.fold_in(jax.random.fold_in(key, 6), axis_at), (parts,), jnp.float32, least / len(cuts), top_value / len(cuts))
        return jnp.repeat(jnp.exp(draws), dims[axis_at] // parts).reshape((-1,) + (1,) * (len(dims) - axis_at - 1))

    loudness = one(*cuts[0])
    for cut in cuts[1:]:
        loudness = loudness * one(*cut)
    return loudness


def distinct(own_key, rows, amount, top, lift):
    sequence = jax.random.permutation(jax.random.fold_in(own_key, 1), amount)
    pull = sequence
    for power in range(3):
        pull = pull * pull // amount
    pull = pull * lift // amount
    tickets = jax.random.randint(jax.random.fold_in(own_key, 2), (rows, amount), 0, 4096) + pull
    fixed_rows = jax.random.permutation(jax.random.fold_in(own_key, 3), rows)[jnp.arange(amount) % rows]
    tickets = jnp.where(jnp.arange(rows)[:, None] == fixed_rows[None, :], 1 << 14, tickets)
    merit = tickets * amount + jnp.arange(amount)
    return lax.top_k(merit.astype(jnp.int32), top)[1].astype(jnp.int32)


def noise(own_key, dims, scale, reach, pieces=(), kind=jnp.bfloat16):
    drawn = jax.random.normal(own_key, dims, jnp.float32) * scale
    if len(pieces) > 0:
        drawn = level_of(own_key, dims, pieces, -0.22, 0.18) * drawn
    return jnp.clip(drawn, min=-reach, max=reach).astype(kind)


def setup_inputs(seed: int = 0) -> dict:
    arg_keys = jax.random.split(jax.random.key(seed), 10)
    return {
        "input_spikes": plant(jax.random.randint(arg_keys[0], (D // 16, ALL_ITEMS), 0, 65536), jax.random.fold_in(arg_keys[0], 1), 0, 65535).astype(jnp.int32),
        "query_spikes": plant(jax.random.randint(arg_keys[1], (HE // 16, ALL_ITEMS), 0, 65536), jax.random.fold_in(arg_keys[1], 1), 0, 65535).astype(jnp.int32),
        "key_spikes": plant(jax.random.randint(arg_keys[2], (HE // 16, ALL_ITEMS), 0, 65536), jax.random.fold_in(arg_keys[2], 1), 0, 65535).astype(jnp.int32),
        "values": noise(arg_keys[3], (ALL_ITEMS, HE), 1.0, 6.0, ((0, 32), (1, 8))),
        "query_slope": jnp.clip(jnp.exp(math.log(2.0) - 2.0794415 * jax.random.uniform(arg_keys[4], (ALL_ITEMS, HE), jnp.float32) ** level_of(arg_keys[4], (ALL_ITEMS, HE), ((0, 32), (1, 8)), -0.2, 0.2)), 0.25, 2.0).astype(jnp.bfloat16),
        "key_slope": jnp.clip(jnp.exp(math.log(2.0) - 2.0794415 * jax.random.uniform(arg_keys[5], (ALL_ITEMS, HE), jnp.float32) ** level_of(arg_keys[5], (ALL_ITEMS, HE), ((0, 32), (1, 8)), -0.2, 0.2)), 0.25, 2.0).astype(jnp.bfloat16),
        "grad_out": noise(arg_keys[6], (ALL_ITEMS, HE), 1.0, 6.0, ((0, 32), (1, 8))),
        "log_gate": draw_log_gate(jax.random.fold_in(arg_keys[9], 71), 0),
        "pattern": distinct(arg_keys[8], NCB, NRB, SEL, 0),
    }


highest = lax.Precision.HIGHEST

def dims_of(left_dim, right_dim):
    return (((left_dim,), (right_dim,)), ((), ()))

def unpack_flags(packed):
    shifts = jnp.arange(16, dtype=jnp.int32)
    flags = jnp.bitwise_and(jnp.right_shift(packed[:, None, :], shifts[None, :, None]), 1)
    return flags.reshape(packed.shape[0] * 16, packed.shape[1]).astype(jnp.bfloat16)

def decay_matrix(cumulative):
    spread = cumulative[:, None] - cumulative[None, :]
    places = jnp.arange(cumulative.shape[0])
    causal = places[:, None] >= places[None, :]
    return jnp.where(causal, jnp.exp(jnp.minimum(spread, 0.0)), 0.0)

def first_phase(query_cols, key_cols, head_values, cumulative):
    decays = decay_matrix(cumulative)
    intersection = lax.dot_general(query_cols, key_cols, dims_of(0, 0), preferred_element_type=jnp.float32)
    weights = intersection * decays
    weights_low = weights.astype(jnp.bfloat16)
    local_num = jnp.dot(weights_low, head_values, preferred_element_type=jnp.float32)
    local_den = lax.optimization_barrier(jnp.sum(weights, axis=1))
    tail_decay = jnp.exp(cumulative[-1] - cumulative)
    key_float = key_cols.astype(jnp.float32) * tail_decay[None, :]
    state_sum = jnp.dot(key_float, head_values.astype(jnp.float32), precision=highest)
    key_sum = lax.optimization_barrier(jnp.sum(key_float, axis=1))
    return (weights_low, local_num, local_den, jnp.exp(cumulative[-1]), state_sum, key_sum)

def second_phase(query_cols, key_cols, head_values, head_grad, cumulative, weights_low, local_num, local_den, state_in, keys_in):
    decays = decay_matrix(cumulative)
    lead_decay = jnp.exp(cumulative)
    query_float = query_cols.astype(jnp.float32)
    carried_num = lax.dot_general(query_float, state_in, dims_of(0, 0), precision=highest)
    numerator = local_num + lead_decay[:, None] * carried_num
    denominator = 1.0 + local_den + lead_decay * jnp.dot(keys_in, query_float, precision=highest)
    output = numerator / denominator[:, None]
    grad_float = head_grad.astype(jnp.float32)
    scaled = grad_float / denominator[:, None]
    norm_grad = -lax.optimization_barrier(jnp.sum(grad_float * output, axis=1)) / denominator
    scaled_low = scaled.astype(jnp.bfloat16)
    cross_term = lax.dot_general(scaled_low, head_values, dims_of(1, 1), preferred_element_type=jnp.float32)
    mixed_low = ((cross_term + norm_grad[:, None]) * decays).astype(jnp.bfloat16)
    carried_query = lax.dot_general(scaled, state_in, dims_of(1, 1), precision=highest) + norm_grad[:, None] * keys_in[None, :]
    grad_query = lax.dot_general(mixed_low, key_cols, dims_of(1, 1), preferred_element_type=jnp.float32) + lead_decay[:, None] * carried_query
    grad_key = lax.dot_general(mixed_low, query_cols, dims_of(0, 1), preferred_element_type=jnp.float32)
    grad_value = lax.dot_general(weights_low, scaled_low, dims_of(0, 0), preferred_element_type=jnp.float32)
    adjoint_sum = jnp.dot(query_float * lead_decay[None, :], scaled, precision=highest)
    adjoint_vec = jnp.dot(query_float, lead_decay * norm_grad, precision=highest)
    return (grad_query, grad_key, grad_value, adjoint_sum, adjoint_vec)

def third_phase(key_cols, head_values, cumulative, grad_key_local, grad_value_local, adjoint, adjoint_vec):
    tail_decay = jnp.exp(cumulative[-1] - cumulative)[:, None]
    value_float = head_values.astype(jnp.float32)
    key_float = key_cols.astype(jnp.float32)
    grad_key = grad_key_local + tail_decay * (lax.dot_general(value_float, adjoint, dims_of(1, 1), precision=highest) + adjoint_vec[None, :])
    grad_value = grad_value_local + tail_decay * lax.dot_general(key_float, adjoint, dims_of(0, 0), precision=highest)
    return (grad_key, grad_value)

def sequence_grads(query_cols, key_cols, head_values, head_grad, head_gate):
    blocks = SPAN_PER_SERIES // TOK_DEV
    query_blocks = query_cols.reshape(HEAD, blocks, TOK_DEV).transpose(1, 0, 2)
    key_blocks = key_cols.reshape(HEAD, blocks, TOK_DEV).transpose(1, 0, 2)
    value_blocks = head_values.reshape(blocks, TOK_DEV, HEAD)
    grad_blocks = head_grad.reshape(blocks, TOK_DEV, HEAD)
    cumulative = jnp.cumsum(head_gate.reshape(blocks, TOK_DEV), axis=1)
    weights_low, local_num, local_den, totals, state_sum, key_sum = jax.vmap(first_phase)(query_blocks, key_blocks, value_blocks, cumulative)

    def forward_step(carried, block_items):
        state_now, keys_now = carried
        decay_total, state_add, keys_add = block_items
        return ((decay_total * state_now + state_add, decay_total * keys_now + keys_add), (state_now, keys_now))
    start_state = (jnp.zeros((HEAD, HEAD), jnp.float32), jnp.zeros((HEAD,), jnp.float32))
    unused, (state_in, keys_in) = lax.scan(forward_step, start_state, (totals, state_sum, key_sum))
    grad_query, grad_key, grad_value, adjoint_sum, adjoint_vec = jax.vmap(second_phase)(query_blocks, key_blocks, value_blocks, grad_blocks, cumulative, weights_low, local_num, local_den, state_in, keys_in)

    def backward_step(carried, block_items):
        adjoint_now, vector_now = carried
        decay_total, adjoint_add, vector_add = block_items
        return ((adjoint_add + decay_total * adjoint_now, vector_add + decay_total * vector_now), (adjoint_now, vector_now))
    unused_end, (adjoint_in, vector_in) = lax.scan(backward_step, start_state, (totals, adjoint_sum, adjoint_vec), reverse=True)
    grad_key, grad_value = jax.vmap(third_phase)(key_blocks, value_blocks, cumulative, grad_key, grad_value, adjoint_in, vector_in)
    return (grad_query.reshape(SPAN_PER_SERIES, HEAD), grad_key.reshape(SPAN_PER_SERIES, HEAD), grad_value.reshape(SPAN_PER_SERIES, HEAD))

def reference(input_spikes, query_spikes, key_spikes, values, query_slope, key_slope, grad_out, log_gate, pattern):
    word_rows = HEAD // 16

    def one_head(head_index):
        head_start = head_index.astype(jnp.int32)
        query_cols = unpack_flags(lax.dynamic_slice_in_dim(query_spikes, head_start * word_rows, word_rows, 0))
        key_cols = unpack_flags(lax.dynamic_slice_in_dim(key_spikes, head_start * word_rows, word_rows, 0))
        head_values = lax.dynamic_slice_in_dim(values, head_start * HEAD, HEAD, 1)
        head_grad = lax.dynamic_slice_in_dim(grad_out, head_start * HEAD, HEAD, 1)
        head_gate = lax.dynamic_slice_in_dim(log_gate, head_start, 1, 0)[0]
        result_sets = []
        for seq_index in range(ALL_ITEMS // SPAN_PER_SERIES):
            first_token = seq_index * SPAN_PER_SERIES
            last_token = first_token + SPAN_PER_SERIES
            result_sets.append(sequence_grads(query_cols[:, first_token:last_token], key_cols[:, first_token:last_token], head_values[first_token:last_token], head_grad[first_token:last_token], head_gate[first_token:last_token]))
        return tuple((jnp.concatenate([result_set[part_index] for result_set in result_sets], axis=0) for part_index in range(3)))
    grad_query, grad_key, grad_value = lax.map(one_head, jnp.arange(ATTENTION_PLANES, dtype=jnp.int32))
    flat_query = grad_query.transpose(1, 0, 2).reshape(ALL_ITEMS, ATTENTION_PLANES * HEAD)
    flat_key = grad_key.transpose(1, 0, 2).reshape(ALL_ITEMS, ATTENTION_PLANES * HEAD)
    query_grad = (query_slope.astype(jnp.float32) * flat_query).astype(jnp.bfloat16)
    key_grad = (key_slope.astype(jnp.float32) * flat_key).astype(jnp.bfloat16)
    value_low = grad_value.transpose(1, 0, 2).reshape(ALL_ITEMS, ATTENTION_PLANES * HEAD).astype(jnp.bfloat16)
    input_blocks = unpack_flags(input_spikes).reshape(D // BLK, BLK, ALL_ITEMS)

    def column_grad(column):
        chosen = jnp.take(input_blocks, pattern[column], axis=0).astype(jnp.float32)
        block_values = lax.dynamic_slice_in_dim(value_low, column.astype(jnp.int32) * BLK, BLK, 1).astype(jnp.float32)
        return jnp.einsum('sat,tb->sab', chosen, block_values, precision=highest).reshape(SEL, BLK * BLK)
    value_grad = lax.map(column_grad, jnp.arange(ATTENTION_PLANES * HEAD // BLK, dtype=jnp.int32))
    return (query_grad, key_grad, value_grad.transpose(1, 0, 2))
```

```python
import functools

import jax
import jax.numpy as jnp
from jax import lax
from jax.experimental import pallas as pl
from jax.experimental.pallas import tpu as pltpu
from jax.sharding import PartitionSpec as P

HEAD = 128
BLK = 64
SEL = 16
MESH = pl.DeviceIdType.MESH
CHUNK = 32
HOP = 5
f32 = jnp.float32
bf16 = jnp.bfloat16


def mm(a, b):
    return lax.dot_general(a, b, (((1,), (0,)), ((), ())), preferred_element_type=f32)


def mm_nt(a, b):
    return lax.dot_general(a, b, (((1,), (1,)), ((), ())), preferred_element_type=f32)


def mm_tn(a, b):
    return lax.dot_general(a, b, (((0,), (0,)), ((), ())), preferred_element_type=f32)


def split(a):
    high = a.astype(bf16)
    return high, (a - high.astype(f32)).astype(bf16)


def mm_exact_left(a, b):
    high, low = split(b)
    return mm(a, high) + mm(a, low)


def bits_of(words, tokens):
    spread = jnp.broadcast_to(words[:, None, :], (HEAD // 16, 16, tokens))
    shifts = lax.broadcasted_iota(jnp.int32, spread.shape, 1)
    flags = jnp.bitwise_and(jnp.right_shift(spread, shifts), 1)
    return flags.reshape(HEAD, tokens).astype(f32).astype(bf16)


def enter(partners):
    barrier = pltpu.get_barrier_semaphore()
    for device in partners:
        pl.semaphore_signal(barrier, inc=1, device_id=device, device_id_type=MESH)
    pl.semaphore_wait(barrier, len(partners))


def attention_kernel(
    n, heads, tokens,
    qw, kw, v, do, gate, qs, ks,
    dq, dk, dv,
    kc, kr, qr, lead, tail, wl, num, rden, gl, gf, decay, dvl,
    yy, s_in, s_out, xx, c_in, c_out,
    send1, ag1, send2, ag2, p_rows,
    s1_send, s1_recv, s2_send, s2_recv, f_send, f_recv, b_send, b_recv,
):
    me = lax.axis_index("ctx")
    chunks = heads * HEAD // CHUNK

    barrier = pltpu.get_barrier_semaphore()

    def greet(i, _):
        pl.semaphore_signal(
            barrier, inc=1, device_id={"ctx": lax.rem(me + i, n)}, device_id_type=MESH
        )
        return 0

    lax.fori_loop(1, n, greet, 0)

    rows = lax.broadcasted_iota(jnp.int32, (tokens, tokens), 0)
    cols = lax.broadcasted_iota(jnp.int32, (tokens, tokens), 1)
    lower = (rows >= cols).astype(f32)
    hi = lax.Precision.HIGHEST
    gates = gate[...]
    run_rows = lax.dot_general(
        gates, lower, (((1,), (1,)), ((), ())), precision=hi, preferred_element_type=f32
    )
    p_rows[0:heads, :] = jnp.exp(
        jnp.broadcast_to(jnp.sum(gates, axis=1, keepdims=True), (heads, HEAD))
    )

    def head_cols(h):
        return pl.ds(pl.multiple_of(h * HEAD, HEAD), HEAD)

    def sums(h, _):
        words = pl.ds(pl.multiple_of(h * (HEAD // 16), HEAD // 16), HEAD // 16)
        keys = bits_of(kw[words, :], tokens)
        kc[h] = keys
        key_rows = keys.T
        kr[h] = key_rows
        qr[h] = bits_of(qw[words, :], tokens).T
        spread = jnp.broadcast_to(gate[pl.ds(h, 1), :], (HEAD, tokens))
        run = lax.dot_general(
            lower, spread, (((1,), (1,)), ((), ())), precision=hi, preferred_element_type=f32
        )
        lead[h] = run
        last = jnp.broadcast_to(run[tokens - 1 : tokens, :], (tokens, HEAD))
        end = jnp.exp(last - run)
        tail[h] = end
        send1[pl.ds(h, 1), :] = jnp.sum(key_rows.astype(f32) * end, axis=0, keepdims=True)
        return 0

    lax.fori_loop(0, heads, sums, 0)
    send1[heads : 2 * heads, :] = p_rows[0:heads, :]
    ag1[me] = send1[...]
    pl.semaphore_wait(barrier, n - 1)

    def gather(send, target, send_sem, recv_sem, i):
        peer = lax.rem(me + i, n)
        return pltpu.make_async_remote_copy(
            src_ref=send,
            dst_ref=target.at[me],
            send_sem=send_sem.at[i],
            recv_sem=recv_sem.at[me],
            device_id={"ctx": peer},
            device_id_type=MESH,
        )

    def arrival(send, target, send_sem, recv_sem, i):
        peer = lax.rem(me + i, n)
        return pltpu.make_async_remote_copy(
            src_ref=send,
            dst_ref=target.at[peer],
            send_sem=send_sem.at[i],
            recv_sem=recv_sem.at[peer],
            device_id={"ctx": peer},
            device_id_type=MESH,
        )

    def start_gather(send, target, send_sem, recv_sem):
        def one(i, _):
            gather(send, target, send_sem, recv_sem, i).start()
            return 0

        lax.fori_loop(1, n, one, 0)

    def end_gather(send, target, send_sem, recv_sem):
        def one(i, _):
            arrival(send, target, send_sem, recv_sem, i).wait_recv()
            return 0

        lax.fori_loop(1, n, one, 0)

    def sent_gather(send, target, send_sem, recv_sem):
        def one(i, _):
            gather(send, target, send_sem, recv_sem, i).wait_send()
            return 0

        lax.fori_loop(1, n, one, 0)

    first = (send1, ag1, s1_send, s1_recv)
    second = (send2, ag2, s2_send, s2_recv)
    start_gather(*first)

    def local_part(h, _):
        run = lead[h]
        run_wide = jnp.concatenate([run, run], axis=1)
        run_row = lax.dot_general(
            jnp.broadcast_to(gate[pl.ds(h, 1), :], (8, tokens)), lower,
            (((1,), (1,)), ((), ())), precision=hi, preferred_element_type=f32,
        )[0:1, :]
        spread = run_wide - jnp.broadcast_to(run_row, (tokens, tokens))
        mask = jnp.where(rows >= cols, jnp.exp(jnp.minimum(spread, 0.0)), 0.0)
        decay[h] = mask
        weights = mm(qr[h], kc[h]) * mask
        low = weights.astype(bf16)
        wl[h] = low
        vh = v[:, head_cols(h)]
        num[h] = mm(low, vh)
        rden[h] = jnp.broadcast_to(jnp.sum(weights, axis=1, keepdims=True), (tokens, HEAD))
        yy[h] = mm_exact_left(kc[h], tail[h] * vh.astype(f32))
        lead[h] = jnp.exp(run)
        return 0

    lax.fori_loop(0, heads, local_part, 0)
    end_gather(*first)

    def carry_keys(i, state):
        item = ag1[i]
        new = item[heads : 2 * heads, :] * state + item[0:heads, :]
        return jnp.where(i < me, new, state)

    send2[...] = lax.fori_loop(0, n, carry_keys, jnp.zeros((heads, HEAD), f32))

    def scaled_part(h, _):
        keys_in = jnp.broadcast_to(send2[pl.ds(h, 1), :], (HEAD, HEAD))
        high, low = split(keys_in)
        q_rows = qr[h]
        met = mm_nt(q_rows, high) + mm_nt(q_rows, low)
        inverse = 1.0 / (1.0 + rden[h] + lead[h] * met)
        rden[h] = inverse
        scaled = do[:, head_cols(h)].astype(f32) * inverse
        gl[h] = scaled.astype(bf16)
        high, low = split(lead[h] * scaled)
        xx[h] = mm_tn(q_rows, high) + mm_tn(q_rows, low)
        return 0

    lax.fori_loop(0, heads, scaled_part, 0)

    @pl.when(me == 0)
    def _():
        s_in[...] = jnp.zeros_like(s_in)

    @pl.when(me == n - 1)
    def _():
        c_in[...] = jnp.zeros_like(c_in)

    per_head = HEAD // CHUNK

    def piece(ref, c):
        start = pl.multiple_of(lax.rem(c, per_head) * CHUNK, CHUNK)
        return ref.at[c // per_head, pl.ds(start, CHUNK), :]

    def onward(out, landing, send_sem, recv_sem, c, peer):
        return pltpu.make_async_remote_copy(
            src_ref=piece(out, c),
            dst_ref=piece(landing, c),
            send_sem=send_sem.at[c],
            recv_sem=recv_sem.at[c],
            device_id={"ctx": peer},
            device_id_type=MESH,
        )

    right, left = lax.rem(me + 1, n), lax.rem(me + n - 1, n)
    lag = 2 * me - (n - 1)
    f_first = jnp.clip(lag * HOP, 0, chunks)
    b_first = jnp.clip(-lag * HOP, 0, chunks)

    def pass_on(c, has_in, has_out, peer, add, landing, out, send_sem, recv_sem):
        copy = onward(out, landing, send_sem, recv_sem, c, peer)

        @pl.when(has_in)
        def _():
            copy.wait_recv()

        @pl.when(has_out)
        def _():
            factor = p_rows[pl.ds(c // per_head, 1), :]
            piece(out, c)[...] = piece(landing, c)[...] * factor + piece(add, c)[...]
            copy.start()

    def turn(s, _):
        cf = s - f_first
        cb = s - b_first

        @pl.when(jnp.logical_and(cf >= 0, cf < chunks))
        def _():
            pass_on(cf, me > 0, me < n - 1, right, yy, s_in, s_out, f_send, f_recv)

        @pl.when(jnp.logical_and(cb >= 0, cb < chunks))
        def _():
            pass_on(cb, me < n - 1, me > 0, left, xx, c_in, c_out, b_send, b_recv)

        return 0

    lax.fori_loop(0, 2 * chunks, turn, 0)

    def carried_part(h, _):
        q_rows, k_rows = qr[h], kr[h]
        high, low = split(s_in[h])
        carried = mm(q_rows, high) + mm(q_rows, low)
        inverse = rden[h]
        begin = lead[h]
        output = (num[h] + begin * carried) * inverse
        given = do[:, head_cols(h)].astype(f32)
        slant = -jnp.sum(given * output, axis=1, keepdims=True)
        slant = jnp.broadcast_to(slant, (tokens, HEAD)) * inverse
        scaled = gl[h]
        vh = v[:, head_cols(h)]
        mixed = mm_nt(scaled, vh) + jnp.concatenate([slant, slant], axis=1)
        mixed = (mixed * decay[h]).astype(bf16)
        keys_in = jnp.broadcast_to(send2[pl.ds(h, 1), :], (tokens, HEAD))
        from_state = mm_nt(scaled, high) + slant * keys_in
        query = mm(mixed, k_rows) + begin * from_state
        dq[:, head_cols(h)] = (qs[:, head_cols(h)].astype(f32) * query).astype(bf16)
        gf[pl.ds(h, 1), :] = jnp.sum(q_rows.astype(f32) * (begin * slant), axis=0, keepdims=True)
        high, low = split(c_in[h])
        end = tail[h]
        num[h] = mm_tn(mixed, q_rows) + end * (mm_nt(vh, high) + mm_nt(vh, low))
        value = mm_tn(wl[h], scaled) + end * (mm(k_rows, high) + mm(k_rows, low))
        dv[:, head_cols(h)] = value.astype(bf16)
        return 0

    lax.fori_loop(0, heads, carried_part, 0)
    ag2[me] = gf[...]
    start_gather(gf, ag2, s2_send, s2_recv)
    end_gather(gf, ag2, s2_send, s2_recv)

    def carry_back(i, state):
        at = n - 1 - i
        new = ag2[at] + ag1[at][heads : 2 * heads, :] * state
        return jnp.where(at > me, new, state)

    send2[...] = lax.fori_loop(0, n, carry_back, jnp.zeros((heads, HEAD), f32))

    def keys_part(h, _):
        vector = jnp.broadcast_to(send2[pl.ds(h, 1), :], (tokens, HEAD))
        key = num[h] + tail[h] * vector
        dk[:, head_cols(h)] = (ks[:, head_cols(h)].astype(f32) * key).astype(bf16)
        return 0

    lax.fori_loop(0, heads, keys_part, 0)
    sent_gather(*first)
    sent_gather(gf, ag2, s2_send, s2_recv)

    @pl.when(me < n - 1)
    def _():
        def one(c, _):
            onward(s_out, s_in, f_send, f_recv, c, right).wait_send()
            return 0

        lax.fori_loop(0, chunks, one, 0)

    @pl.when(me > 0)
    def _():
        def one(c, _):
            onward(c_out, c_in, b_send, b_recv, c, left).wait_send()
            return 0

        lax.fori_loop(0, chunks, one, 0)


def attention(qw, kw, v, do, gate, qs, ks):
    tokens, width = v.shape
    heads = width // HEAD
    n = lax.axis_size("ctx")
    chunks = heads * HEAD // CHUNK
    flat = jax.ShapeDtypeStruct((tokens, width), bf16)
    vm = pl.BlockSpec(memory_space=pltpu.VMEM)
    by_head = lambda a, b, t: pltpu.VMEM((heads, a, b), t)
    return pl.pallas_call(
        functools.partial(attention_kernel, n, heads, tokens),
        out_shape=(flat, flat, flat),
        in_specs=[vm] * 7,
        out_specs=(vm, vm, vm),
        scratch_shapes=[
            by_head(HEAD, tokens, bf16),
            by_head(tokens, HEAD, bf16),
            by_head(tokens, HEAD, bf16),
            by_head(tokens, HEAD, f32),
            by_head(tokens, HEAD, f32),
            by_head(tokens, tokens, bf16),
            by_head(tokens, HEAD, f32),
            by_head(tokens, HEAD, f32),
            by_head(tokens, HEAD, bf16),
            pltpu.VMEM((heads, HEAD), f32),
            by_head(tokens, tokens, f32),
            pltpu.VMEM((8, 128), f32),
            by_head(HEAD, HEAD, f32),
            by_head(HEAD, HEAD, f32),
            by_head(HEAD, HEAD, f32),
            by_head(HEAD, HEAD, f32),
            by_head(HEAD, HEAD, f32),
            by_head(HEAD, HEAD, f32),
            pltpu.VMEM((2 * heads, HEAD), f32),
            pltpu.VMEM((n, 2 * heads, HEAD), f32),
            pltpu.VMEM((heads, HEAD), f32),
            pltpu.VMEM((n, heads, HEAD), f32),
            pltpu.VMEM((heads, HEAD), f32),
            pltpu.SemaphoreType.DMA((n,)),
            pltpu.SemaphoreType.DMA((n,)),
            pltpu.SemaphoreType.DMA((n,)),
            pltpu.SemaphoreType.DMA((n,)),
            pltpu.SemaphoreType.DMA((chunks,)),
            pltpu.SemaphoreType.DMA((chunks,)),
            pltpu.SemaphoreType.DMA((chunks,)),
            pltpu.SemaphoreType.DMA((chunks,)),
        ],
        compiler_params=pltpu.CompilerParams(
            collective_id=0, has_side_effects=True, vmem_limit_bytes=40 << 20
        ),
        name="attention",
    )(qw, kw, v, do, gate, qs, ks)


def partial_kernel(
    slots, columns, tokens, pattern, xw, dv, out, xu, lhs, rhs
):
    half = BLK // 2
    words = xw.shape[0]
    step = 64

    def open_bits(i, _):
        at = pl.multiple_of(i * step, step)
        spread = jnp.broadcast_to(xw[pl.ds(at, step), :][:, None, :], (step, 8, tokens))
        shifts = 2 * lax.broadcasted_iota(jnp.int32, spread.shape, 1)
        even = jnp.bitwise_and(jnp.right_shift(spread, shifts), 1)
        odd = jnp.bitwise_and(jnp.right_shift(spread, shifts + 1), 1)
        to = pl.ds(pl.multiple_of(at * 8, step * 8), step * 8)
        xu[to, 0:tokens] = even.reshape(step * 8, tokens).astype(f32).astype(bf16)
        xu[to, tokens : 2 * tokens] = odd.reshape(step * 8, tokens).astype(f32).astype(bf16)
        return 0

    lax.fori_loop(0, words // step, open_bits, 0)

    def one_head(h, _):
        pair = dv[:, pl.ds(pl.multiple_of(h * HEAD, HEAD), HEAD)].astype(f32)
        turned = pltpu.roll(pair, BLK, axis=1)
        left = lax.broadcasted_iota(jnp.int32, pair.shape, 1) < BLK
        zero = jnp.zeros_like(pair)
        for k in range(2):
            upper, lower = (pair, turned) if k == 0 else (turned, pair)
            rhs[0:tokens, :] = jnp.where(left, upper, zero).astype(bf16)
            rhs[tokens : 2 * tokens, :] = jnp.where(left, zero, lower).astype(bf16)
            j = 2 * h + k
            for s in range(slots):
                block = pl.multiple_of(pattern[j, s] * half, half)
                lhs[s * half : (s + 1) * half, :] = xu[pl.ds(block, half), :]
            result = mm(lhs[...], rhs[...])
            for s in range(slots):
                out[s, j] = result[s * half : (s + 1) * half, :]
        return 0

    lax.fori_loop(0, columns // 2, one_head, 0)


def partials(xw, dv, pattern):
    words, tokens = xw.shape
    columns, slots = pattern.shape
    half = BLK // 2
    vm = pl.BlockSpec(memory_space=pltpu.VMEM)
    return pl.pallas_call(
        functools.partial(partial_kernel, slots, columns, tokens),
        out_shape=jax.ShapeDtypeStruct((slots, columns, half, HEAD), f32),
        in_specs=[pl.BlockSpec(memory_space=pltpu.SMEM), vm, vm],
        out_specs=vm,
        scratch_shapes=[
            pltpu.VMEM((words * 8, 2 * tokens), bf16),
            pltpu.VMEM((slots * half, 2 * tokens), bf16),
            pltpu.VMEM((2 * tokens, HEAD), bf16),
        ],
        compiler_params=pltpu.CompilerParams(vmem_limit_bytes=32 << 20),
        name="partials",
    )(pattern, xw, dv)


def sum_kernel(
    nz, columns, half,
    part, out,
    zbuf, ybuf, abuf, bbuf, mine, theirs,
    zs, zr, ys, yr, as_, ar, bs, br, es, er,
):
    ctx = lax.axis_index("ctx")
    dp = lax.axis_index("dp")
    z = lax.rem(ctx, nz)
    y_hi = ctx // nz
    y = 2 * y_hi + dp
    ny = 4
    first = columns // 2
    quarter = columns // 4

    def at_z(k):
        return {"ctx": y_hi * nz + lax.rem(z + k + nz, nz)}

    def at_y(k):
        other = lax.rem(y + k + ny, ny)
        return {"dp": lax.rem(other, 2), "ctx": (other // 2) * nz + z}

    barrier = pltpu.get_barrier_semaphore()
    partners = [at_z(k) for k in range(1, nz)] + [at_y(k) for k in range(1, ny)]
    for device in partners:
        pl.semaphore_signal(barrier, inc=1, device_id=device, device_id_type=MESH)
    pl.semaphore_wait(barrier, len(partners))

    def copy(src, dst, send, recv, device):
        return pltpu.make_async_remote_copy(
            src_ref=src, dst_ref=dst, send_sem=send, recv_sem=recv,
            device_id=device, device_id_type=MESH,
        )

    zsub, ysub = 4, 4
    zc = first // zsub

    def z_slot(direction, k):
        if direction == 0:
            return lax.rem(z - 1 - k + 2 * nz, nz)
        return nz + lax.rem(z + 1 + k, nz)

    def z_copy(direction, k, c):
        if k == 0:
            src = part.at[z_slot(direction, 0), pl.ds(c * zc, zc)]
        else:
            src = zbuf.at[direction, k - 1, pl.ds(c * zc, zc)]
        return copy(
            src, zbuf.at[direction, k, pl.ds(c * zc, zc)],
            zs.at[direction, k, c], zr.at[direction, k, c],
            at_z(1 if direction == 0 else -1),
        )

    def z_take(direction, k, c):
        z_copy(direction, k, c).wait_recv()
        where = (direction, k, pl.ds(c * zc, zc))
        own = part[z_slot(direction, k + 1), pl.ds(c * zc, zc)]
        zbuf[where] = zbuf[where] + own

    def y_place(direction, k, c):
        step = -1 - k if direction == 0 else 1 + k
        to = lax.rem(y + step + 2 * ny, ny)
        slot = (to // 2) * nz + direction * (nz // 2) + c
        return slot, pl.multiple_of(first + quarter * lax.rem(to, 2), quarter)

    def y_copy(direction, k, c):
        if k == 0:
            slot, col = y_place(direction, 0, c)
            src = part.at[slot, pl.ds(col, quarter)]
        else:
            src = ybuf.at[k - 1, direction * (nz // 2) + c]
        return copy(
            src, ybuf.at[k, direction * (nz // 2) + c],
            ys.at[direction, k, c], yr.at[direction, k, c],
            at_y(1 if direction == 0 else -1),
        )

    def y_take(direction, k, c):
        y_copy(direction, k, c).wait_recv()
        slot, col = y_place(direction, k + 1, c)
        where = (k, direction * (nz // 2) + c)
        ybuf[where] = ybuf[where] + part[slot, pl.ds(col, quarter)]

    for c in range(max(zsub, ysub)):
        for direction in (0, 1):
            if c < zsub:
                z_copy(direction, 0, c).start()
            if c < ysub:
                y_copy(direction, 0, c).start()

    events = []
    for k in range(nz - 1):
        for c in range(zsub):
            events.append((k + c / zsub, 0, k, c))
    for k in range(ny - 1):
        for c in range(ysub):
            events.append((2 * k + 2 * c / ysub + 0.9, 1, k, c))
    events.sort()
    for _, kind, k, c in events:
        for direction in (0, 1):
            if kind == 0:
                z_take(direction, k, c)
                if k < nz - 2:
                    z_copy(direction, k + 1, c).start()
            else:
                y_take(direction, k, c)
                if k < ny - 2:
                    y_copy(direction, k + 1, c).start()

    def a_copy(k):
        to = lax.rem(y + k, ny)
        col = pl.multiple_of(quarter * lax.rem(to, 2), quarter)
        return copy(
            zbuf.at[to // 2, nz - 2, pl.ds(col, quarter)], abuf.at[k],
            as_.at[k], ar.at[k], at_y(k),
        )

    def b_copy(k):
        return copy(
            ybuf.at[ny - 2, lax.rem(z + k, nz)], bbuf.at[k], bs.at[k], br.at[k], at_z(k)
        )

    a_copies = [a_copy(k) for k in range(1, ny)]
    b_copies = [b_copy(k) for k in range(1, nz)]
    for c in a_copies + b_copies:
        c.start()
    col = pl.multiple_of(quarter * dp, quarter)
    mine[0] = zbuf[y_hi, nz - 2, pl.ds(col, quarter)]
    mine[1] = ybuf[ny - 2, z]
    for k, c in enumerate(a_copies):
        c.wait_recv()
        mine[0] = mine[0] + abuf[k + 1]
    for k, c in enumerate(b_copies):
        c.wait_recv()
        mine[1] = mine[1] + bbuf[k + 1]
    swap = copy(mine, theirs, es.at[0], er.at[0], {"dp": 1 - dp})
    swap.start()
    swap.wait_recv()

    for part_at in range(2):
        own = mine[part_at]
        other = theirs[part_at]
        low = jnp.where(dp == 0, own, other)
        high = jnp.where(dp == 0, other, own)
        out[2 * part_at * quarter : (2 * part_at + 1) * quarter] = low
        out[(2 * part_at + 1) * quarter : (2 * part_at + 2) * quarter] = high

    swap.wait_send()
    for c in a_copies + b_copies:
        c.wait_send()
    for direction in (0, 1):
        for k in range(nz - 1):
            for c in range(zsub):
                z_copy(direction, k, c).wait_send()
        for k in range(ny - 1):
            for c in range(ysub):
                y_copy(direction, k, c).wait_send()


def sum_parts(part):
    slots, columns, half, lanes = part.shape
    nz = lax.axis_size("ctx") // 2
    ny = 4
    vm = pl.BlockSpec(memory_space=pltpu.VMEM)
    dma = pltpu.SemaphoreType.DMA
    return pl.pallas_call(
        functools.partial(sum_kernel, nz, columns, half),
        out_shape=jax.ShapeDtypeStruct((columns, half, lanes), f32),
        in_specs=[vm],
        out_specs=vm,
        scratch_shapes=[
            pltpu.VMEM((2, nz - 1, columns // 2, half, lanes), f32),
            pltpu.VMEM((ny - 1, nz, columns // 4, half, lanes), f32),
            pltpu.VMEM((ny, columns // 4, half, lanes), f32),
            pltpu.VMEM((nz, columns // 4, half, lanes), f32),
            pltpu.VMEM((2, columns // 4, half, lanes), f32),
            pltpu.VMEM((2, columns // 4, half, lanes), f32),
            dma((2, nz - 1, 4)), dma((2, nz - 1, 4)),
            dma((2, ny - 1, 4)), dma((2, ny - 1, 4)),
            dma((ny,)), dma((ny,)), dma((nz,)), dma((nz,)), dma((1,)), dma((1,)),
        ],
        compiler_params=pltpu.CompilerParams(
            collective_id=1, has_side_effects=True, vmem_limit_bytes=32 << 20
        ),
        name="sum_parts",
    )(part)


def per_device(
    input_spikes, query_spikes, key_spikes, values, query_slope, key_slope, grad_out, log_gate, pattern
):
    query_grad, key_grad, value_low = attention(
        query_spikes, key_spikes, values, grad_out, log_gate, query_slope, key_slope
    )
    part = partials(input_spikes, value_low, pattern)
    summed = sum_parts(part)
    return (query_grad, key_grad, summed.reshape(1, pattern.shape[0], BLK * BLK))


def solution(mesh):
    column = P("tensor", ("dp", "ctx"))
    token = P(("dp", "ctx"), "tensor")
    in_specs = (
        P(None, ("dp", "ctx")), column, column, token, token, token, token, column, P("tensor", None)
    )
    return jax.shard_map(
        per_device,
        mesh=mesh,
        in_specs=in_specs,
        out_specs=(token, token, P("ctx", "tensor", None)),
        check_vma=False,
    )
```

```python
import functools
import types

import jax
import jax.numpy as jnp
from jax import lax
from jax.experimental import pallas as pl
from jax.experimental.pallas import tpu as pltpu
from jax.sharding import PartitionSpec as P

HEAD = 128
BLK = 64
SEL = 16
MESH = pl.DeviceIdType.MESH
CHUNK = 32
HOP = 5
CROSS = 8
f32 = jnp.float32
bf16 = jnp.bfloat16


def mm(a, b):
    return lax.dot_general(a, b, (((1,), (0,)), ((), ())), preferred_element_type=f32)


def mm_nt(a, b):
    return lax.dot_general(a, b, (((1,), (1,)), ((), ())), preferred_element_type=f32)


def mm_tn(a, b):
    return lax.dot_general(a, b, (((0,), (0,)), ((), ())), preferred_element_type=f32)


def split(a):
    high = a.astype(bf16)
    return high, (a - high.astype(f32)).astype(bf16)


def mm_exact_left(a, b):
    high, low = split(b)
    return mm(a, high) + mm(a, low)


def bits_of(words, tokens):
    spread = jnp.broadcast_to(words[:, None, :], (HEAD // 16, 16, tokens))
    shifts = lax.broadcasted_iota(jnp.int32, spread.shape, 1)
    flags = jnp.bitwise_and(jnp.right_shift(spread, shifts), 1)
    return flags.reshape(HEAD, tokens).astype(f32).astype(bf16)


def copy_to(src, dst, send, recv, device):
    return pltpu.make_async_remote_copy(
        src_ref=src, dst_ref=dst, send_sem=send, recv_sem=recv,
        device_id=device, device_id_type=MESH,
    )


def kernel(n, heads, tokens, columns, slots, names, pattern, *refs):
    r = types.SimpleNamespace(**dict(zip(names, refs)))
    me = lax.axis_index("ctx")
    dp = lax.axis_index("dp")
    nz, ny = n // 2, 4
    z, y_hi = lax.rem(me, nz), me // nz
    y = 2 * y_hi + dp
    chunks = heads * HEAD // CHUNK
    per_head = HEAD // CHUNK
    half = BLK // 2

    def at_ctx(k):
        return {"ctx": k}

    def at_z(k):
        return {"ctx": y_hi * nz + lax.rem(z + k + nz, nz)}

    def at_y(k):
        other = lax.rem(y + k + ny, ny)
        return {"dp": lax.rem(other, 2), "ctx": (other // 2) * nz + z}

    barrier = pltpu.get_barrier_semaphore()

    def greet(i, _):
        pl.semaphore_signal(
            barrier, inc=1, device_id=at_ctx(lax.rem(me + i, n)), device_id_type=MESH
        )
        return 0

    lax.fori_loop(1, n, greet, 0)
    for k in (1, 3):
        pl.semaphore_signal(barrier, inc=1, device_id=at_y(k), device_id_type=MESH)

    loads = {}
    for i, name in enumerate(("gate", "kw", "qw", "v", "do", "xw", "qs", "ks")):
        loads[name] = pltpu.make_async_copy(
            getattr(r, name + "_h"), getattr(r, name), r.in_sem.at[i]
        )
        loads[name].start()

    rows = lax.broadcasted_iota(jnp.int32, (tokens, tokens), 0)
    cols = lax.broadcasted_iota(jnp.int32, (tokens, tokens), 1)
    lower = (rows >= cols).astype(f32)
    hi = lax.Precision.HIGHEST
    loads["gate"].wait()
    gates = r.gate[...]
    r.send1[heads : 2 * heads, :] = jnp.exp(
        jnp.broadcast_to(jnp.sum(gates, axis=1, keepdims=True), (heads, HEAD))
    )
    loads["kw"].wait()

    def head_cols(h):
        return pl.ds(pl.multiple_of(h * HEAD, HEAD), HEAD)

    def head_words(h):
        return pl.ds(pl.multiple_of(h * (HEAD // 16), HEAD // 16), HEAD // 16)

    def sums(h, _):
        keys = bits_of(r.kw[head_words(h), :], tokens)
        r.kc[h] = keys
        key_rows = keys.T
        r.kr[h] = key_rows
        spread = jnp.broadcast_to(r.gate[pl.ds(h, 1), :], (HEAD, tokens))
        run = lax.dot_general(
            lower, spread, (((1,), (1,)), ((), ())), precision=hi, preferred_element_type=f32
        )
        r.lead[h] = run
        last = jnp.broadcast_to(run[tokens - 1 : tokens, :], (tokens, HEAD))
        end = jnp.exp(last - run)
        r.tail[h] = end
        r.send1[pl.ds(h, 1), :] = jnp.sum(key_rows.astype(f32) * end, axis=0, keepdims=True)
        return 0

    lax.fori_loop(0, heads, sums, 0)
    r.ag1[me] = r.send1[...]
    pl.semaphore_wait(barrier, n + 1)

    def gather(send, target, send_sem, recv_sem, i):
        peer = lax.rem(me + i, n)
        return copy_to(send, target.at[me], send_sem.at[i], recv_sem.at[me], at_ctx(peer))

    def arrival(send, target, send_sem, recv_sem, i):
        peer = lax.rem(me + i, n)
        return copy_to(send, target.at[peer], send_sem.at[i], recv_sem.at[peer], at_ctx(peer))

    def start_gather(*which):
        def one(i, _):
            gather(*which, i).start()
            return 0

        lax.fori_loop(1, n, one, 0)

    def end_gather(*which):
        def one(i, _):
            arrival(*which, i).wait_recv()
            return 0

        lax.fori_loop(1, n, one, 0)

    def sent_gather(*which):
        def one(i, _):
            gather(*which, i).wait_send()
            return 0

        lax.fori_loop(1, n, one, 0)

    first_gather = (r.send1, r.ag1, r.s1_send, r.s1_recv)
    second_gather = (r.gf, r.ag2, r.s2_send, r.s2_recv)
    start_gather(*first_gather)
    loads["qw"].wait()
    loads["v"].wait()

    def local_part(h, _):
        r.qr[h] = bits_of(r.qw[head_words(h), :], tokens).T
        run = r.lead[h]
        run_wide = jnp.concatenate([run, run], axis=1)
        run_row = lax.dot_general(
            jnp.broadcast_to(r.gate[pl.ds(h, 1), :], (8, tokens)), lower,
            (((1,), (1,)), ((), ())), precision=hi, preferred_element_type=f32,
        )[0:1, :]
        spread = run_wide - jnp.broadcast_to(run_row, (tokens, tokens))
        mask = jnp.where(rows >= cols, jnp.exp(jnp.minimum(spread, 0.0)), 0.0)
        r.decay[h] = mask
        weights = mm(r.qr[h], r.kc[h]) * mask
        low = weights.astype(bf16)
        r.wl[h] = low
        vh = r.v[:, head_cols(h)]
        r.num[h] = mm(low, vh)
        r.rden[h] = jnp.broadcast_to(jnp.sum(weights, axis=1, keepdims=True), (tokens, HEAD))
        r.yy[h] = mm_exact_left(r.kc[h], r.tail[h] * vh.astype(f32))
        r.lead[h] = jnp.exp(run)
        return 0

    lax.fori_loop(0, heads, local_part, 0)
    end_gather(*first_gather)

    def carry_keys(i, state):
        keys, down, up = state
        item = r.ag1[i]
        factor = item[heads : 2 * heads, :]
        keys = jnp.where(i < me, factor * keys + item[0:heads, :], keys)
        down = jnp.where(jnp.logical_and(i > me, i < nz), down * factor, down)
        up = jnp.where(jnp.logical_and(i < me, i >= nz), up * factor, up)
        return keys, down, up

    ones = jnp.ones((heads, HEAD), f32)
    keys, down, up = lax.fori_loop(0, n, carry_keys, (jnp.zeros((heads, HEAD), f32), ones, ones))
    r.keys_in[...] = keys
    r.down[...] = jnp.where(y_hi == 0, down, 0.0)
    r.up[...] = jnp.where(y_hi == 1, up, 0.0)
    loads["do"].wait()

    def scaled_part(h, _):
        keys_in = jnp.broadcast_to(r.keys_in[pl.ds(h, 1), :], (HEAD, HEAD))
        high, low = split(keys_in)
        q_rows = r.qr[h]
        met = mm_nt(q_rows, high) + mm_nt(q_rows, low)
        inverse = 1.0 / (1.0 + r.rden[h] + r.lead[h] * met)
        r.rden[h] = inverse
        scaled = r.do[:, head_cols(h)].astype(f32) * inverse
        r.gl[h] = scaled.astype(bf16)
        high, low = split(r.lead[h] * scaled)
        r.xx[h] = mm_tn(q_rows, high) + mm_tn(q_rows, low)
        return 0

    lax.fori_loop(0, heads, scaled_part, 0)
    loads["xw"].wait()

    @pl.when(z == 0)
    def _():
        r.s_in[...] = jnp.zeros_like(r.s_in)

    @pl.when(z == nz - 1)
    def _():
        r.c_in[...] = jnp.zeros_like(r.c_in)

    def piece(ref, c):
        start = pl.multiple_of(lax.rem(c, per_head) * CHUNK, CHUNK)
        return ref.at[c // per_head, pl.ds(start, CHUNK), :]

    def entry(line, group):
        near = jnp.where(line == 1, nz - 1, 0)
        return jnp.where(group == 0, near, nz - 1 - near)

    def line_copy(forward, c):
        out, landing, send, recv, step = (
            (r.s_out, r.s_in, r.f_send, r.f_recv, 1)
            if forward
            else (r.c_out, r.c_in, r.b_send, r.b_recv, -1)
        )
        return copy_to(piece(out, c), piece(landing, c), send.at[c], recv.at[c], at_z(step))

    def cross_copy(forward, c):
        out, send = (r.s_out, r.f_send) if forward else (r.c_out, r.b_send)
        line = 1 if forward else 0
        at = line * nz + entry(line, c // (chunks // 2))
        return copy_to(piece(out, c), piece(r.total, c), send.at[c], r.t_recv.at[c], at_ctx(at))

    def pass_line(forward, c):
        last = (nz - 1) if forward else 0
        has_in = z > 0 if forward else z < nz - 1
        onward = z != last
        crossing = jnp.logical_and(z == last, y_hi == (0 if forward else 1))
        landing, out, add = (r.s_in, r.s_out, r.yy) if forward else (r.c_in, r.c_out, r.xx)

        @pl.when(has_in)
        def _():
            line_copy(forward, c).wait_recv()

        @pl.when(jnp.logical_or(onward, crossing))
        def _():
            factor = r.send1[pl.ds(heads + c // per_head, 1), :]
            piece(out, c)[...] = piece(landing, c)[...] * factor + piece(add, c)[...]

        @pl.when(onward)
        def _():
            line_copy(forward, c).start()

        @pl.when(crossing)
        def _():
            cross_copy(forward, c).start()

    def total_copy(c, step):
        send = r.t_send_down if step < 0 else r.t_send_up
        return copy_to(piece(r.total, c), piece(r.total, c), send.at[c], r.t_recv.at[c], at_z(step))

    def distances(group):
        e = entry(y_hi, group)
        return lax.rem(e - z + nz, nz), lax.rem(z - e + nz, nz)

    def pass_total(group, c):
        below, above = distances(group)
        total_copy(c, -1).wait_recv()

        @pl.when(below < nz // 2)
        def _():
            total_copy(c, -1).start()

        @pl.when(above < nz // 2 - 1)
        def _():
            total_copy(c, 1).start()

    step_words = r.xw.shape[0] // heads

    def side_part(h):
        r.dvl[h] = mm_tn(r.wl[h], r.gl[h])
        at = pl.multiple_of(h * step_words, step_words)
        spread = jnp.broadcast_to(
            r.xw[pl.ds(at, step_words), :][:, None, :], (step_words, 8, tokens)
        )
        shifts = 2 * lax.broadcasted_iota(jnp.int32, spread.shape, 1)
        even = jnp.bitwise_and(jnp.right_shift(spread, shifts), 1)
        odd = jnp.bitwise_and(jnp.right_shift(spread, shifts + 1), 1)
        count = step_words * 8 // half
        to = pl.ds(h * count, count)
        r.xu[to, :, 0:tokens] = even.reshape(count, half, tokens).astype(f32).astype(bf16)
        r.xu[to, :, tokens : 2 * tokens] = odd.reshape(count, half, tokens).astype(f32).astype(bf16)

    f_off = z * HOP
    b_off = (nz - 1 - z) * HOP
    t_off = []
    for group in range(2):
        below, above = distances(group)
        t_off.append(
            (nz - 1) * HOP + CROSS + jnp.minimum(below, above) * HOP + group * (chunks // 2)
        )
    side_off = jnp.where(z < nz // 2, 0, chunks)
    steps = (nz - 1) * HOP + CROSS + nz // 2 * HOP + chunks

    def turn(s, _):
        for group in range(2):
            ct = s - t_off[group]

            @pl.when(jnp.logical_and(ct >= 0, ct < chunks // 2))
            def _():
                pass_total(group, ct + group * (chunks // 2))

        cb = s - b_off

        @pl.when(jnp.logical_and(cb >= 0, cb < chunks))
        def _():
            pass_line(False, cb)

        cf = s - f_off

        @pl.when(jnp.logical_and(cf >= 0, cf < chunks))
        def _():
            pass_line(True, cf)

        cs = s - side_off

        @pl.when(jnp.logical_and(cs >= 0, cs < heads))
        def _():
            side_part(cs)

        return 0

    lax.fori_loop(0, steps, turn, 0)

    def product_part(h, _):
        adjoint = r.c_in[h] + r.down[pl.ds(h, 1), :] * r.total[h]
        r.c_in[h] = adjoint
        high, low = split(adjoint)
        k_rows = r.kr[h]
        value = r.dvl[h] + r.tail[h] * (mm(k_rows, high) + mm(k_rows, low))
        pair = value.astype(bf16).astype(f32)
        turned = pltpu.roll(pair, BLK, axis=1)
        left = lax.broadcasted_iota(jnp.int32, pair.shape, 1) < BLK
        zero = jnp.zeros_like(pair)
        for k in range(2):
            upper, under = (pair, turned) if k == 0 else (turned, pair)
            r.rhs[0:tokens, :] = jnp.where(left, upper, zero).astype(bf16)
            r.rhs[tokens : 2 * tokens, :] = jnp.where(left, zero, under).astype(bf16)
            j = 2 * h + k
            for s in range(slots):
                r.lhs[s * half : (s + 1) * half, :] = r.xu[pattern[j, s]]
            result = mm(r.lhs[...], r.rhs[...])
            for s in range(slots):
                r.part[s, j] = result[s * half : (s + 1) * half, :]
        return 0

    def carried_part(h):
        q_rows, k_rows = r.qr[h], r.kr[h]
        high, low = split(r.s_in[h] + r.up[pl.ds(h, 1), :] * r.total[h])
        carried = mm(q_rows, high) + mm(q_rows, low)
        inverse = r.rden[h]
        begin = r.lead[h]
        output = (r.num[h] + begin * carried) * inverse
        given = r.do[:, head_cols(h)].astype(f32)
        slant = -jnp.sum(given * output, axis=1, keepdims=True)
        slant = jnp.broadcast_to(slant, (tokens, HEAD)) * inverse
        scaled = r.gl[h]
        vh = r.v[:, head_cols(h)]
        mixed = mm_nt(scaled, vh) + jnp.concatenate([slant, slant], axis=1)
        mixed = (mixed * r.decay[h]).astype(bf16)
        keys_in = jnp.broadcast_to(r.keys_in[pl.ds(h, 1), :], (tokens, HEAD))
        from_state = mm_nt(scaled, high) + slant * keys_in
        query = mm(mixed, k_rows) + begin * from_state
        r.dq[:, head_cols(h)] = (r.qs[:, head_cols(h)].astype(f32) * query).astype(bf16)
        r.gf[pl.ds(h, 1), :] = jnp.sum(q_rows.astype(f32) * (begin * slant), axis=0, keepdims=True)
        high, low = split(r.c_in[h])
        r.num[h] = mm_tn(mixed, q_rows) + r.tail[h] * (mm_nt(vh, high) + mm_nt(vh, low))

    def second_start():
        r.ag2[me] = r.gf[...]
        start_gather(*second_gather)

    def keys_end():
        end_gather(*second_gather)

        def carry_back(i, state):
            at = n - 1 - i
            new = r.ag2[at] + r.ag1[at][heads : 2 * heads, :] * state
            return jnp.where(at > me, new, state)

        r.keys_in[...] = lax.fori_loop(0, n, carry_back, jnp.zeros((heads, HEAD), f32))

        def keys_part(h, _):
            vector = jnp.broadcast_to(r.keys_in[pl.ds(h, 1), :], (tokens, HEAD))
            key = r.num[h] + r.tail[h] * vector
            r.dk[:, head_cols(h)] = (r.ks[:, head_cols(h)].astype(f32) * key).astype(bf16)
            return 0

        lax.fori_loop(0, heads, keys_part, 0)

    part, zbuf, ybuf = r.part, r.zbuf, r.ybuf
    first, quarter = columns // 2, columns // 4
    zsub = ysub = 4
    zc = first // zsub

    def z_slot(direction, k):
        if direction == 0:
            return lax.rem(z - 1 - k + 2 * nz, nz)
        return nz + lax.rem(z + 1 + k, nz)

    def z_copy(direction, k, c):
        if k == 0:
            src = part.at[z_slot(direction, 0), pl.ds(c * zc, zc)]
        else:
            src = zbuf.at[direction, k - 1, pl.ds(c * zc, zc)]
        return copy_to(
            src, zbuf.at[direction, k, pl.ds(c * zc, zc)],
            r.zs.at[direction, k, c], r.zr.at[direction, k, c],
            at_z(1 if direction == 0 else -1),
        )

    def z_take(direction, k, c):
        z_copy(direction, k, c).wait_recv()
        where = (direction, k, pl.ds(c * zc, zc))
        zbuf[where] = zbuf[where] + part[z_slot(direction, k + 1), pl.ds(c * zc, zc)]

    def y_place(direction, k, c):
        step = -1 - k if direction == 0 else 1 + k
        to = lax.rem(y + step + 2 * ny, ny)
        slot = (to // 2) * nz + direction * (nz // 2) + c
        return slot, pl.multiple_of(first + quarter * lax.rem(to, 2), quarter)

    def y_copy(direction, k, c):
        if k == 0:
            slot, col = y_place(direction, 0, c)
            src = part.at[slot, pl.ds(col, quarter)]
        else:
            src = ybuf.at[k - 1, direction * (nz // 2) + c]
        return copy_to(
            src, ybuf.at[k, direction * (nz // 2) + c],
            r.ys.at[direction, k, c], r.yr.at[direction, k, c],
            at_y(1 if direction == 0 else -1),
        )

    def y_take(direction, k, c):
        y_copy(direction, k, c).wait_recv()
        slot, col = y_place(direction, k + 1, c)
        where = (k, direction * (nz // 2) + c)
        ybuf[where] = ybuf[where] + part[slot, pl.ds(col, quarter)]

    lax.fori_loop(0, heads // 2, product_part, 0)
    for c in range(zsub):
        for direction in (0, 1):
            z_copy(direction, 0, c).start()
    lax.fori_loop(heads // 2, heads, product_part, 0)
    for c in range(ysub):
        for direction in (0, 1):
            y_copy(direction, 0, c).start()
    loads["qs"].wait()
    loads["ks"].wait()

    events = []
    for k in range(nz - 1):
        for c in range(zsub):
            events.append((k + c / zsub, 0, k, c))
    for k in range(ny - 1):
        for c in range(ysub):
            events.append((2 * k + 2 * c / ysub + 0.9, 1, k, c))
    for h in range(heads):
        events.append((0.3 + 4.0 * h / heads, 2, h, 0))
    events.append((4.3, 3, 0, 0))
    events.sort()
    for _, kind, k, c in events:
        if kind == 2:
            carried_part(k)
            continue
        if kind == 3:
            second_start()
            continue
        for direction in (0, 1):
            if kind == 0:
                z_take(direction, k, c)
                if k < nz - 2:
                    z_copy(direction, k + 1, c).start()
            else:
                y_take(direction, k, c)
                if k < ny - 2:
                    y_copy(direction, k + 1, c).start()

    def a_copy(k):
        to = lax.rem(y + k, ny)
        col = pl.multiple_of(quarter * lax.rem(to, 2), quarter)
        return copy_to(
            zbuf.at[to // 2, nz - 2, pl.ds(col, quarter)], r.abuf.at[k],
            r.as_.at[k], r.ar.at[k], at_y(k),
        )

    def b_copy(k):
        return copy_to(
            ybuf.at[ny - 2, lax.rem(z + k, nz)], r.bbuf.at[k], r.bs.at[k], r.br.at[k], at_z(k)
        )

    a_copies = [a_copy(k) for k in range(1, ny)]
    b_copies = [b_copy(k) for k in range(1, nz)]
    for c in b_copies + a_copies:
        c.start()
    keys_end()
    mine, theirs = r.mine, r.theirs
    col = pl.multiple_of(quarter * dp, quarter)
    mine[0] = zbuf[y_hi, nz - 2, pl.ds(col, quarter)]
    mine[1] = ybuf[ny - 2, z]
    for k, c in enumerate(a_copies):
        c.wait_recv()
        mine[0] = mine[0] + r.abuf[k + 1]
    for k, c in enumerate(b_copies):
        c.wait_recv()
        mine[1] = mine[1] + r.bbuf[k + 1]
    swap = copy_to(mine, theirs, r.es.at[0], r.er.at[0], {"dp": 1 - dp})
    swap.start()
    swap.wait_recv()

    for k in range(2):
        own, other = mine[k], theirs[k]
        r.out[2 * k * quarter : (2 * k + 1) * quarter] = jnp.where(dp == 0, own, other)
        r.out[(2 * k + 1) * quarter : (2 * k + 2) * quarter] = jnp.where(dp == 0, other, own)

    swap.wait_send()
    for c in a_copies + b_copies:
        c.wait_send()
    for direction in (0, 1):
        for k in range(nz - 1):
            for c in range(zsub):
                z_copy(direction, k, c).wait_send()
        for k in range(ny - 1):
            for c in range(ysub):
                y_copy(direction, k, c).wait_send()
    sent_gather(*first_gather)
    sent_gather(*second_gather)

    @pl.when(jnp.logical_or(z < nz - 1, y_hi == 0))
    def _():
        def one(c, _):
            line_copy(True, c).wait_send()
            return 0

        lax.fori_loop(0, chunks, one, 0)

    @pl.when(jnp.logical_or(z > 0, y_hi == 1))
    def _():
        def one(c, _):
            line_copy(False, c).wait_send()
            return 0

        lax.fori_loop(0, chunks, one, 0)

    for group in range(2):
        below, above = distances(group)
        span = (group * (chunks // 2), (group + 1) * (chunks // 2))

        @pl.when(below < nz // 2)
        def _():
            def one(c, _):
                total_copy(c, -1).wait_send()
                return 0

            lax.fori_loop(*span, one, 0)

        @pl.when(above < nz // 2 - 1)
        def _():
            def one(c, _):
                total_copy(c, 1).wait_send()
                return 0

            lax.fori_loop(*span, one, 0)


def per_device(xw, qw, kw, v, qs, ks, do, gate, pattern):
    tokens, width = v.shape
    heads = width // HEAD
    words = xw.shape[0]
    columns, slots = pattern.shape
    n = lax.axis_size("ctx")
    nz, ny = n // 2, 4
    chunks = heads * HEAD // CHUNK
    half = BLK // 2
    flat = jax.ShapeDtypeStruct((tokens, width), bf16)
    vmem, dma = pltpu.VMEM, pltpu.SemaphoreType.DMA
    scratch = dict(
        gate=vmem(gate.shape, f32),
        kw=vmem(kw.shape, jnp.int32),
        qw=vmem(qw.shape, jnp.int32),
        v=vmem(v.shape, bf16),
        do=vmem(v.shape, bf16),
        xw=vmem(xw.shape, jnp.int32),
        qs=vmem(v.shape, bf16),
        ks=vmem(v.shape, bf16),
        in_sem=dma((8,)),
        kc=vmem((heads, HEAD, tokens), bf16),
        kr=vmem((heads, tokens, HEAD), bf16),
        qr=vmem((heads, tokens, HEAD), bf16),
        gl=vmem((heads, tokens, HEAD), bf16),
        wl=vmem((heads, tokens, tokens), bf16),
        decay=vmem((heads, tokens, tokens), f32),
        xu=vmem((words * 8 // half, half, 2 * tokens), bf16),
        lhs=vmem((slots * half, 2 * tokens), bf16),
        rhs=vmem((2 * tokens, HEAD), bf16),
        part=vmem((slots, columns, half, HEAD), f32),
        send1=vmem((2 * heads, HEAD), f32),
        ag1=vmem((n, 2 * heads, HEAD), f32),
        ag2=vmem((n, heads, HEAD), f32),
        zbuf=vmem((2, nz - 1, columns // 2, half, HEAD), f32),
        ybuf=vmem((ny - 1, nz, columns // 4, half, HEAD), f32),
        abuf=vmem((ny, columns // 4, half, HEAD), f32),
        bbuf=vmem((nz, columns // 4, half, HEAD), f32),
        mine=vmem((2, columns // 4, half, HEAD), f32),
        theirs=vmem((2, columns // 4, half, HEAD), f32),
        zs=dma((2, nz - 1, 4)),
        zr=dma((2, nz - 1, 4)),
        ys=dma((2, ny - 1, 4)),
        yr=dma((2, ny - 1, 4)),
        as_=dma((ny,)),
        ar=dma((ny,)),
        bs=dma((nz,)),
        br=dma((nz,)),
        es=dma((1,)),
        er=dma((1,)),
    )
    for name in ("lead", "tail", "num", "rden", "dvl"):
        scratch[name] = vmem((heads, tokens, HEAD), f32)
    for name in ("yy", "s_in", "s_out", "xx", "c_in", "c_out", "total"):
        scratch[name] = vmem((heads, HEAD, HEAD), f32)
    for name in ("gf", "keys_in", "down", "up"):
        scratch[name] = vmem((heads, HEAD), f32)
    for name in ("s1_send", "s1_recv", "s2_send", "s2_recv"):
        scratch[name] = dma((n,))
    for name in ("f_send", "f_recv", "b_send", "b_recv", "t_recv", "t_send_up", "t_send_down"):
        scratch[name] = dma((chunks,))
    arguments = ("xw_h", "qw_h", "kw_h", "v_h", "do_h", "gate_h", "qs_h", "ks_h")
    names = arguments + ("dq", "dk", "out") + tuple(scratch)
    whole = pl.BlockSpec(memory_space=pltpu.VMEM)
    dq, dk, out = pl.pallas_call(
        functools.partial(kernel, n, heads, tokens, columns, slots, names),
        out_shape=(flat, flat, jax.ShapeDtypeStruct((columns, half, HEAD), f32)),
        in_specs=[pl.BlockSpec(memory_space=pltpu.SMEM)] + [pl.BlockSpec(memory_space=pl.ANY)] * 8,
        out_specs=(whole, whole, whole),
        scratch_shapes=list(scratch.values()),
        compiler_params=pltpu.CompilerParams(
            collective_id=0, has_side_effects=True, vmem_limit_bytes=60 << 20
        ),
        name="layer",
    )(pattern, xw, qw, kw, v, do, gate, qs, ks)
    return dq, dk, out.reshape(1, columns, BLK * BLK)


def solution(mesh):
    column = P("tensor", ("dp", "ctx"))
    token = P(("dp", "ctx"), "tensor")
    in_specs = (
        P(None, ("dp", "ctx")), column, column, token, token, token, token, column, P("tensor", None)
    )
    return jax.shard_map(
        per_device,
        mesh=mesh,
        in_specs=in_specs,
        out_specs=(token, token, P("ctx", "tensor", None)),
        check_vma=False,
    )
```

```python
import functools
import types

import jax
import jax.numpy as jnp
from jax import lax
from jax.experimental import pallas as pl
from jax.experimental.pallas import tpu as pltpu
from jax.sharding import PartitionSpec as P

HEAD = 128
BLK = 64
SEL = 16
MESH = pl.DeviceIdType.MESH
CHUNK = 32
HOP = 8
CROSS = 12
f32 = jnp.float32
bf16 = jnp.bfloat16


def mm(a, b):
    return lax.dot_general(a, b, (((1,), (0,)), ((), ())), preferred_element_type=f32)


def mm_nt(a, b):
    return lax.dot_general(a, b, (((1,), (1,)), ((), ())), preferred_element_type=f32)


def mm_tn(a, b):
    return lax.dot_general(a, b, (((0,), (0,)), ((), ())), preferred_element_type=f32)


def split(a):
    high = a.astype(bf16)
    return high, (a - high.astype(f32)).astype(bf16)


def split3(a):
    high = a.astype(bf16)
    rest = a - high.astype(f32)
    return (high, *split(rest))


def mm_exact_left(a, b):
    high, low = split(b)
    return mm(a, high) + mm(a, low)


def bits_of(words, tokens):
    spread = jnp.broadcast_to(words[:, None, :], (HEAD // 16, 16, tokens))
    shifts = lax.broadcasted_iota(jnp.int32, spread.shape, 1)
    flags = jnp.bitwise_and(jnp.right_shift(spread, shifts), 1)
    return flags.reshape(HEAD, tokens).astype(f32).astype(bf16)


def copy_to(src, dst, send, recv, device):
    return pltpu.make_async_remote_copy(
        src_ref=src, dst_ref=dst, send_sem=send, recv_sem=recv,
        device_id=device, device_id_type=MESH,
    )


def kernel(n, heads, tokens, columns, slots, names, pattern, *refs):
    r = types.SimpleNamespace(**dict(zip(names, refs)))
    me = lax.axis_index("ctx")
    dp = lax.axis_index("dp")
    nz, ny = n // 2, 4
    z, y_hi = lax.rem(me, nz), me // nz
    y = 2 * y_hi + dp
    chunks = heads * HEAD // CHUNK
    per_head = HEAD // CHUNK
    half = BLK // 2

    def at_ctx(k):
        return {"ctx": k}

    def at_z(k):
        return {"ctx": y_hi * nz + lax.rem(z + k + nz, nz)}

    def at_y(k):
        other = lax.rem(y + k + ny, ny)
        return {"dp": lax.rem(other, 2), "ctx": (other // 2) * nz + z}

    barrier = pltpu.get_barrier_semaphore()

    def greet(i, _):
        pl.semaphore_signal(
            barrier, inc=1, device_id=at_ctx(lax.rem(me + i, n)), device_id_type=MESH
        )
        return 0

    lax.fori_loop(1, n, greet, 0)
    for k in (1, 3):
        pl.semaphore_signal(barrier, inc=1, device_id=at_y(k), device_id_type=MESH)

    loads = {}
    for i, name in enumerate(("gate", "kw", "qw", "v", "do", "xw", "qs", "ks")):
        loads[name] = pltpu.make_async_copy(
            getattr(r, name + "_h"), getattr(r, name), r.in_sem.at[i]
        )
        loads[name].start()

    rows = lax.broadcasted_iota(jnp.int32, (tokens, tokens), 0)
    cols = lax.broadcasted_iota(jnp.int32, (tokens, tokens), 1)
    lower = jnp.where(rows >= cols, 1.0, 0.0)
    lower_bits = lower.astype(bf16)
    loads["gate"].wait()
    gates = r.gate[...]
    r.send1[heads : 2 * heads, :] = jnp.exp(
        jnp.broadcast_to(jnp.sum(gates, axis=1, keepdims=True), (heads, HEAD))
    )
    r.run_rows[...] = lax.dot_general(
        gates, lower, (((1,), (1,)), ((), ())),
        precision=lax.Precision.HIGHEST, preferred_element_type=f32,
    )
    loads["kw"].wait()

    def head_cols(h):
        return pl.ds(pl.multiple_of(h * HEAD, HEAD), HEAD)

    def head_words(h):
        return pl.ds(pl.multiple_of(h * (HEAD // 16), HEAD // 16), HEAD // 16)

    def sums(h, _):
        keys = bits_of(r.kw[head_words(h), :], tokens)
        r.kc[h] = keys
        key_rows = keys.T
        r.kr[h] = key_rows
        spread = jnp.broadcast_to(r.gate[pl.ds(h, 1), :], (HEAD, tokens))
        run = sum(mm_nt(lower_bits, part) for part in split3(spread))
        r.lead[h] = run
        last = jnp.broadcast_to(run[tokens - 1 : tokens, :], (tokens, HEAD))
        end = jnp.exp(last - run)
        r.tail[h] = end
        r.send1[pl.ds(h, 1), :] = jnp.sum(key_rows.astype(f32) * end, axis=0, keepdims=True)
        return 0

    lax.fori_loop(0, heads, sums, 0)
    r.ag1[me] = r.send1[...]
    pl.semaphore_wait(barrier, n + 1)

    def gather(send, target, send_sem, recv_sem, i):
        peer = lax.rem(me + i, n)
        return copy_to(send, target.at[me], send_sem.at[i], recv_sem.at[me], at_ctx(peer))

    def arrival(send, target, send_sem, recv_sem, i):
        peer = lax.rem(me + i, n)
        return copy_to(send, target.at[peer], send_sem.at[i], recv_sem.at[peer], at_ctx(peer))

    def start_gather(*which):
        def one(i, _):
            gather(*which, i).start()
            return 0

        lax.fori_loop(1, n, one, 0)

    def end_gather(*which):
        def one(i, _):
            arrival(*which, i).wait_recv()
            return 0

        lax.fori_loop(1, n, one, 0)

    def sent_gather(*which):
        def one(i, _):
            gather(*which, i).wait_send()
            return 0

        lax.fori_loop(1, n, one, 0)

    first_gather = (r.send1, r.ag1, r.s1_send, r.s1_recv)
    second_gather = (r.gf, r.ag2, r.s2_send, r.s2_recv)
    start_gather(*first_gather)
    loads["qw"].wait()
    loads["v"].wait()

    def local_part(h, _):
        r.qr[h] = bits_of(r.qw[head_words(h), :], tokens).T
        run = r.lead[h]
        run_wide = jnp.concatenate([run, run], axis=1)
        spread = run_wide - jnp.broadcast_to(r.run_rows[pl.ds(h, 1), :], (tokens, tokens))
        mask = jnp.where(rows >= cols, jnp.exp(jnp.minimum(spread, 0.0)), 0.0)
        r.decay[h] = mask
        weights = mm(r.qr[h], r.kc[h]) * mask
        low = weights.astype(bf16)
        r.wl[h] = low
        vh = r.v[:, head_cols(h)]
        r.num[h] = mm(low, vh)
        r.rden[h] = jnp.broadcast_to(jnp.sum(weights, axis=1, keepdims=True), (tokens, HEAD))
        r.yy[h] = mm_exact_left(r.kc[h], r.tail[h] * vh.astype(f32))
        r.lead[h] = jnp.exp(run)
        return 0

    lax.fori_loop(0, heads, local_part, 0)
    end_gather(*first_gather)

    def carry_keys(i, state):
        keys, down, up = state
        item = r.ag1[i]
        factor = item[heads : 2 * heads, :]
        keys = jnp.where(i < me, factor * keys + item[0:heads, :], keys)
        down = jnp.where(jnp.logical_and(i > me, i < nz), down * factor, down)
        up = jnp.where(jnp.logical_and(i < me, i >= nz), up * factor, up)
        return keys, down, up

    ones = jnp.ones((heads, HEAD), f32)
    keys, down, up = lax.fori_loop(0, n, carry_keys, (jnp.zeros((heads, HEAD), f32), ones, ones))
    r.keys_in[...] = keys
    r.down[...] = jnp.where(y_hi == 0, down, 0.0)
    r.up[...] = jnp.where(y_hi == 1, up, 0.0)
    loads["do"].wait()

    def scaled_part(h, _):
        keys_in = jnp.broadcast_to(r.keys_in[pl.ds(h, 1), :], (HEAD, HEAD))
        high, low = split(keys_in)
        q_rows = r.qr[h]
        met = mm_nt(q_rows, high) + mm_nt(q_rows, low)
        inverse = 1.0 / (1.0 + r.rden[h] + r.lead[h] * met)
        r.rden[h] = inverse
        scaled = r.do[:, head_cols(h)].astype(f32) * inverse
        r.gl[h] = scaled.astype(bf16)
        high, low = split(r.lead[h] * scaled)
        r.xx[h] = mm_tn(q_rows, high) + mm_tn(q_rows, low)
        return 0

    lax.fori_loop(0, heads, scaled_part, 0)
    loads["xw"].wait()

    @pl.when(z == 0)
    def _():
        r.s_in[...] = jnp.zeros_like(r.s_in)

    @pl.when(z == nz - 1)
    def _():
        r.c_in[...] = jnp.zeros_like(r.c_in)

    def piece(ref, c):
        start = pl.multiple_of(lax.rem(c, per_head) * CHUNK, CHUNK)
        return ref.at[c // per_head, pl.ds(start, CHUNK), :]

    def entry(line, group):
        near = jnp.where(line == 1, nz - 1, 0)
        return jnp.where(group == 0, near, nz - 1 - near)

    def line_copy(forward, c):
        out, landing, send, recv, step = (
            (r.s_out, r.s_in, r.f_send, r.f_recv, 1)
            if forward
            else (r.c_out, r.c_in, r.b_send, r.b_recv, -1)
        )
        return copy_to(piece(out, c), piece(landing, c), send.at[c], recv.at[c], at_z(step))

    def cross_copy(forward, c):
        out, send = (r.s_out, r.f_send) if forward else (r.c_out, r.b_send)
        line = 1 if forward else 0
        at = line * nz + entry(line, c // (chunks // 2))
        return copy_to(piece(out, c), piece(r.total, c), send.at[c], r.t_recv.at[c], at_ctx(at))

    def pass_line(forward, c):
        last = (nz - 1) if forward else 0
        has_in = z > 0 if forward else z < nz - 1
        onward = z != last
        crossing = jnp.logical_and(z == last, y_hi == (0 if forward else 1))
        landing, out, add = (r.s_in, r.s_out, r.yy) if forward else (r.c_in, r.c_out, r.xx)

        @pl.when(has_in)
        def _():
            line_copy(forward, c).wait_recv()

        @pl.when(jnp.logical_or(onward, crossing))
        def _():
            factor = r.send1[pl.ds(heads + c // per_head, 1), :]
            piece(out, c)[...] = piece(landing, c)[...] * factor + piece(add, c)[...]

        @pl.when(onward)
        def _():
            line_copy(forward, c).start()

        @pl.when(crossing)
        def _():
            cross_copy(forward, c).start()

    def total_copy(c, step):
        send = r.t_send_down if step < 0 else r.t_send_up
        return copy_to(piece(r.total, c), piece(r.total, c), send.at[c], r.t_recv.at[c], at_z(step))

    def distances(group):
        e = entry(y_hi, group)
        return lax.rem(e - z + nz, nz), lax.rem(z - e + nz, nz)

    def pass_total(group, c):
        below, above = distances(group)
        total_copy(c, -1).wait_recv()

        @pl.when(below < nz // 2)
        def _():
            total_copy(c, -1).start()

        @pl.when(above < nz // 2 - 1)
        def _():
            total_copy(c, 1).start()

    step_words = r.xw.shape[0] // heads

    def side_part(h):
        r.dvl[h] = mm_tn(r.wl[h], r.gl[h])
        at = pl.multiple_of(h * step_words, step_words)
        spread = jnp.broadcast_to(
            r.xw[pl.ds(at, step_words), :][:, None, :], (step_words, 8, tokens)
        )
        shifts = 2 * lax.broadcasted_iota(jnp.int32, spread.shape, 1)
        even = jnp.bitwise_and(jnp.right_shift(spread, shifts), 1)
        odd = jnp.bitwise_and(jnp.right_shift(spread, shifts + 1), 1)
        count = step_words * 8 // half
        to = pl.ds(h * count, count)
        r.xu[to, :, 0:tokens] = even.reshape(count, half, tokens).astype(f32).astype(bf16)
        r.xu[to, :, tokens : 2 * tokens] = odd.reshape(count, half, tokens).astype(f32).astype(bf16)

    f_off = z * HOP
    b_off = (nz - 1 - z) * HOP
    t_off = []
    for group in range(2):
        below, above = distances(group)
        t_off.append(
            (nz - 1) * HOP + CROSS + jnp.minimum(below, above) * HOP + group * (chunks // 2)
        )
    side_off = jnp.where(z < nz // 2, 0, chunks)
    steps = (nz - 1) * HOP + CROSS + nz // 2 * HOP + chunks

    def turn(s, _):
        for group in range(2):
            ct = s - t_off[group]

            @pl.when(jnp.logical_and(ct >= 0, ct < chunks // 2))
            def _():
                pass_total(group, ct + group * (chunks // 2))

        cb = s - b_off

        @pl.when(jnp.logical_and(cb >= 0, cb < chunks))
        def _():
            pass_line(False, cb)

        cf = s - f_off

        @pl.when(jnp.logical_and(cf >= 0, cf < chunks))
        def _():
            pass_line(True, cf)

        cs = s - side_off

        @pl.when(jnp.logical_and(cs >= 0, cs < heads))
        def _():
            side_part(cs)

        return 0

    lax.fori_loop(0, steps, turn, 0)

    def product_part(h, _):
        adjoint = r.c_in[h] + r.down[pl.ds(h, 1), :] * r.total[h]
        r.c_in[h] = adjoint
        high, low = split(adjoint)
        k_rows = r.kr[h]
        value = r.dvl[h] + r.tail[h] * (mm(k_rows, high) + mm(k_rows, low))
        pair = value.astype(bf16).astype(f32)
        turned = pltpu.roll(pair, BLK, axis=1)
        left = lax.broadcasted_iota(jnp.int32, pair.shape, 1) < BLK
        zero = jnp.zeros_like(pair)
        for k in range(2):
            upper, under = (pair, turned) if k == 0 else (turned, pair)
            r.rhs[0:tokens, :] = jnp.where(left, upper, zero).astype(bf16)
            r.rhs[tokens : 2 * tokens, :] = jnp.where(left, zero, under).astype(bf16)
            j = 2 * h + k
            for s in range(slots):
                r.lhs[s * half : (s + 1) * half, :] = r.xu[pattern[j, s]]
            result = mm(r.lhs[...], r.rhs[...])
            for s in range(slots):
                r.part[s, j] = result[s * half : (s + 1) * half, :]
        return 0

    def carried_part(h):
        q_rows, k_rows = r.qr[h], r.kr[h]
        high, low = split(r.s_in[h] + r.up[pl.ds(h, 1), :] * r.total[h])
        carried = mm(q_rows, high) + mm(q_rows, low)
        inverse = r.rden[h]
        begin = r.lead[h]
        output = (r.num[h] + begin * carried) * inverse
        given = r.do[:, head_cols(h)].astype(f32)
        slant = -jnp.sum(given * output, axis=1, keepdims=True)
        slant = jnp.broadcast_to(slant, (tokens, HEAD)) * inverse
        scaled = r.gl[h]
        vh = r.v[:, head_cols(h)]
        mixed = mm_nt(scaled, vh) + jnp.concatenate([slant, slant], axis=1)
        mixed = (mixed * r.decay[h]).astype(bf16)
        keys_in = jnp.broadcast_to(r.keys_in[pl.ds(h, 1), :], (tokens, HEAD))
        from_state = mm_nt(scaled, high) + slant * keys_in
        query = mm(mixed, k_rows) + begin * from_state
        r.dq[:, head_cols(h)] = (r.qs[:, head_cols(h)].astype(f32) * query).astype(bf16)
        r.gf[pl.ds(h, 1), :] = jnp.sum(q_rows.astype(f32) * (begin * slant), axis=0, keepdims=True)
        high, low = split(r.c_in[h])
        r.num[h] = mm_tn(mixed, q_rows) + r.tail[h] * (mm_nt(vh, high) + mm_nt(vh, low))

    def second_start():
        r.ag2[me] = r.gf[...]
        start_gather(*second_gather)

    def keys_end():
        end_gather(*second_gather)

        def carry_back(i, state):
            at = n - 1 - i
            new = r.ag2[at] + r.ag1[at][heads : 2 * heads, :] * state
            return jnp.where(at > me, new, state)

        r.keys_in[...] = lax.fori_loop(0, n, carry_back, jnp.zeros((heads, HEAD), f32))

        def keys_part(h, _):
            vector = jnp.broadcast_to(r.keys_in[pl.ds(h, 1), :], (tokens, HEAD))
            key = r.num[h] + r.tail[h] * vector
            r.dk[:, head_cols(h)] = (r.ks[:, head_cols(h)].astype(f32) * key).astype(bf16)
            return 0

        lax.fori_loop(0, heads, keys_part, 0)

    part, zbuf, ybuf = r.part, r.zbuf, r.ybuf
    first, quarter = columns // 2, columns // 4
    zsub = ysub = 4
    zc = first // zsub

    def z_slot(direction, k):
        if direction == 0:
            return lax.rem(z - 1 - k + 2 * nz, nz)
        return nz + lax.rem(z + 1 + k, nz)

    def z_copy(direction, k, c):
        if k == 0:
            src = part.at[z_slot(direction, 0), pl.ds(c * zc, zc)]
        else:
            src = zbuf.at[direction, k - 1, pl.ds(c * zc, zc)]
        return copy_to(
            src, zbuf.at[direction, k, pl.ds(c * zc, zc)],
            r.zs.at[direction, k, c], r.zr.at[direction, k, c],
            at_z(1 if direction == 0 else -1),
        )

    def z_take(direction, k, c):
        z_copy(direction, k, c).wait_recv()
        where = (direction, k, pl.ds(c * zc, zc))
        zbuf[where] = zbuf[where] + part[z_slot(direction, k + 1), pl.ds(c * zc, zc)]

    def y_place(direction, k, c):
        step = -1 - k if direction == 0 else 1 + k
        to = lax.rem(y + step + 2 * ny, ny)
        slot = (to // 2) * nz + direction * (nz // 2) + c
        return slot, pl.multiple_of(first + quarter * lax.rem(to, 2), quarter)

    def y_copy(direction, k, c):
        if k == 0:
            slot, col = y_place(direction, 0, c)
            src = part.at[slot, pl.ds(col, quarter)]
        else:
            src = ybuf.at[k - 1, direction * (nz // 2) + c]
        return copy_to(
            src, ybuf.at[k, direction * (nz // 2) + c],
            r.ys.at[direction, k, c], r.yr.at[direction, k, c],
            at_y(1 if direction == 0 else -1),
        )

    def y_take(direction, k, c):
        y_copy(direction, k, c).wait_recv()
        slot, col = y_place(direction, k + 1, c)
        where = (k, direction * (nz // 2) + c)
        ybuf[where] = ybuf[where] + part[slot, pl.ds(col, quarter)]

    lax.fori_loop(0, heads // 2, product_part, 0)
    for c in range(zsub):
        for direction in (0, 1):
            z_copy(direction, 0, c).start()
    lax.fori_loop(heads // 2, heads, product_part, 0)
    for c in range(ysub):
        for direction in (0, 1):
            y_copy(direction, 0, c).start()
    loads["qs"].wait()
    loads["ks"].wait()

    events = []
    for k in range(nz - 1):
        for c in range(zsub):
            events.append((k + c / zsub, 0, k, c))
    for k in range(ny - 1):
        for c in range(ysub):
            events.append((2 * k + 2 * c / ysub + 0.9, 1, k, c))
    for h in range(heads):
        events.append((0.3 + 4.0 * h / heads, 2, h, 0))
    events.append((4.3, 3, 0, 0))
    events.sort()
    for _, kind, k, c in events:
        if kind == 2:
            carried_part(k)
            continue
        if kind == 3:
            second_start()
            continue
        for direction in (0, 1):
            if kind == 0:
                z_take(direction, k, c)
                if k < nz - 2:
                    z_copy(direction, k + 1, c).start()
            else:
                y_take(direction, k, c)
                if k < ny - 2:
                    y_copy(direction, k + 1, c).start()

    def a_copy(k):
        to = lax.rem(y + k, ny)
        col = pl.multiple_of(quarter * lax.rem(to, 2), quarter)
        return copy_to(
            zbuf.at[to // 2, nz - 2, pl.ds(col, quarter)], r.abuf.at[k],
            r.as_.at[k], r.ar.at[k], at_y(k),
        )

    def b_copy(k):
        return copy_to(
            ybuf.at[ny - 2, lax.rem(z + k, nz)], r.bbuf.at[k], r.bs.at[k], r.br.at[k], at_z(k)
        )

    a_copies = [a_copy(k) for k in range(1, ny)]
    b_copies = [b_copy(k) for k in range(1, nz)]
    for c in b_copies + a_copies:
        c.start()
    keys_end()
    mine, theirs = r.mine, r.theirs
    col = pl.multiple_of(quarter * dp, quarter)
    mine[0] = zbuf[y_hi, nz - 2, pl.ds(col, quarter)]
    mine[1] = ybuf[ny - 2, z]
    for k, c in enumerate(a_copies):
        c.wait_recv()
        mine[0] = mine[0] + r.abuf[k + 1]
    for k, c in enumerate(b_copies):
        c.wait_recv()
        mine[1] = mine[1] + r.bbuf[k + 1]
    swap = copy_to(mine, theirs, r.es.at[0], r.er.at[0], {"dp": 1 - dp})
    swap.start()
    swap.wait_recv()

    for k in range(2):
        own, other = mine[k], theirs[k]
        low, high = 2 * k * quarter, (2 * k + 1) * quarter
        r.blocks[low : low + quarter] = jnp.where(dp == 0, own, other)
        r.blocks[high : high + quarter] = jnp.where(dp == 0, other, own)
    for k in range(half):
        r.out[:, k * HEAD : (k + 1) * HEAD] = r.blocks[:, k, :]

    swap.wait_send()
    for c in a_copies + b_copies:
        c.wait_send()
    for direction in (0, 1):
        for k in range(nz - 1):
            for c in range(zsub):
                z_copy(direction, k, c).wait_send()
        for k in range(ny - 1):
            for c in range(ysub):
                y_copy(direction, k, c).wait_send()
    sent_gather(*first_gather)
    sent_gather(*second_gather)

    @pl.when(jnp.logical_or(z < nz - 1, y_hi == 0))
    def _():
        def one(c, _):
            line_copy(True, c).wait_send()
            return 0

        lax.fori_loop(0, chunks, one, 0)

    @pl.when(jnp.logical_or(z > 0, y_hi == 1))
    def _():
        def one(c, _):
            line_copy(False, c).wait_send()
            return 0

        lax.fori_loop(0, chunks, one, 0)

    for group in range(2):
        below, above = distances(group)
        span = (group * (chunks // 2), (group + 1) * (chunks // 2))

        @pl.when(below < nz // 2)
        def _():
            def one(c, _):
                total_copy(c, -1).wait_send()
                return 0

            lax.fori_loop(*span, one, 0)

        @pl.when(above < nz // 2 - 1)
        def _():
            def one(c, _):
                total_copy(c, 1).wait_send()
                return 0

            lax.fori_loop(*span, one, 0)


def per_device(xw, qw, kw, v, qs, ks, do, gate, pattern):
    tokens, width = v.shape
    heads = width // HEAD
    words = xw.shape[0]
    columns, slots = pattern.shape
    n = lax.axis_size("ctx")
    nz, ny = n // 2, 4
    chunks = heads * HEAD // CHUNK
    half = BLK // 2
    flat = jax.ShapeDtypeStruct((tokens, width), bf16)
    vmem, dma = pltpu.VMEM, pltpu.SemaphoreType.DMA
    scratch = dict(
        gate=vmem(gate.shape, f32),
        kw=vmem(kw.shape, jnp.int32),
        qw=vmem(qw.shape, jnp.int32),
        v=vmem(v.shape, bf16),
        do=vmem(v.shape, bf16),
        xw=vmem(xw.shape, jnp.int32),
        qs=vmem(v.shape, bf16),
        ks=vmem(v.shape, bf16),
        in_sem=dma((8,)),
        kc=vmem((heads, HEAD, tokens), bf16),
        kr=vmem((heads, tokens, HEAD), bf16),
        qr=vmem((heads, tokens, HEAD), bf16),
        gl=vmem((heads, tokens, HEAD), bf16),
        wl=vmem((heads, tokens, tokens), bf16),
        decay=vmem((heads, tokens, tokens), f32),
        xu=vmem((words * 8 // half, half, 2 * tokens), bf16),
        lhs=vmem((slots * half, 2 * tokens), bf16),
        rhs=vmem((2 * tokens, HEAD), bf16),
        part=vmem((slots, columns, half, HEAD), f32),
        send1=vmem((2 * heads, HEAD), f32),
        ag1=vmem((n, 2 * heads, HEAD), f32),
        ag2=vmem((n, heads, HEAD), f32),
        zbuf=vmem((2, nz - 1, columns // 2, half, HEAD), f32),
        ybuf=vmem((ny - 1, nz, columns // 4, half, HEAD), f32),
        abuf=vmem((ny, columns // 4, half, HEAD), f32),
        bbuf=vmem((nz, columns // 4, half, HEAD), f32),
        mine=vmem((2, columns // 4, half, HEAD), f32),
        theirs=vmem((2, columns // 4, half, HEAD), f32),
        blocks=vmem((columns, half, HEAD), f32),
        run_rows=vmem((heads, tokens), f32),
        zs=dma((2, nz - 1, 4)),
        zr=dma((2, nz - 1, 4)),
        ys=dma((2, ny - 1, 4)),
        yr=dma((2, ny - 1, 4)),
        as_=dma((ny,)),
        ar=dma((ny,)),
        bs=dma((nz,)),
        br=dma((nz,)),
        es=dma((1,)),
        er=dma((1,)),
    )
    for name in ("lead", "tail", "num", "rden", "dvl"):
        scratch[name] = vmem((heads, tokens, HEAD), f32)
    for name in ("yy", "s_in", "s_out", "xx", "c_in", "c_out", "total"):
        scratch[name] = vmem((heads, HEAD, HEAD), f32)
    for name in ("gf", "keys_in", "down", "up"):
        scratch[name] = vmem((heads, HEAD), f32)
    for name in ("s1_send", "s1_recv", "s2_send", "s2_recv"):
        scratch[name] = dma((n,))
    for name in ("f_send", "f_recv", "b_send", "b_recv", "t_recv", "t_send_up", "t_send_down"):
        scratch[name] = dma((chunks,))
    arguments = ("xw_h", "qw_h", "kw_h", "v_h", "do_h", "gate_h", "qs_h", "ks_h")
    names = arguments + ("dq", "dk", "out") + tuple(scratch)
    whole = pl.BlockSpec(memory_space=pltpu.VMEM)
    dq, dk, out = pl.pallas_call(
        functools.partial(kernel, n, heads, tokens, columns, slots, names),
        out_shape=(flat, flat, jax.ShapeDtypeStruct((columns, BLK * BLK), f32)),
        in_specs=[pl.BlockSpec(memory_space=pltpu.SMEM)] + [pl.BlockSpec(memory_space=pl.ANY)] * 8,
        out_specs=(whole, whole, whole),
        scratch_shapes=list(scratch.values()),
        compiler_params=pltpu.CompilerParams(
            collective_id=0, has_side_effects=True, vmem_limit_bytes=60 << 20
        ),
        name="layer",
    )(pattern, xw, qw, kw, v, do, gate, qs, ks)
    return dq, dk, out.reshape(1, columns, BLK * BLK)


def solution(mesh):
    column = P("tensor", ("dp", "ctx"))
    token = P(("dp", "ctx"), "tensor")
    in_specs = (
        P(None, ("dp", "ctx")), column, column, token, token, token, token, column, P("tensor", None)
    )
    return jax.shard_map(
        per_device,
        mesh=mesh,
        in_specs=in_specs,
        out_specs=(token, token, P("ctx", "tensor", None)),
        check_vma=False,
    )
```

```python
import functools
import types

import jax
import jax.numpy as jnp
from jax import lax
from jax.experimental import pallas as pl
from jax.experimental.pallas import tpu as pltpu
from jax.sharding import PartitionSpec as P

HEAD = 128
BLK = 64
SEL = 16
MESH = pl.DeviceIdType.MESH
CHUNK = 32
HOP = 8
CROSS = 12
f32 = jnp.float32
bf16 = jnp.bfloat16


def mm(a, b):
    return lax.dot_general(a, b, (((1,), (0,)), ((), ())), preferred_element_type=f32)


def mm_nt(a, b):
    return lax.dot_general(a, b, (((1,), (1,)), ((), ())), preferred_element_type=f32)


def mm_tn(a, b):
    return lax.dot_general(a, b, (((0,), (0,)), ((), ())), preferred_element_type=f32)


def split(a):
    high = a.astype(bf16)
    return high, (a - high.astype(f32)).astype(bf16)


def split3(a):
    high = a.astype(bf16)
    rest = a - high.astype(f32)
    return (high, *split(rest))


def mm_exact_left(a, b):
    high, low = split(b)
    return mm(a, high) + mm(a, low)


def bits_of(words, tokens):
    spread = jnp.broadcast_to(words[:, None, :], (HEAD // 16, 16, tokens))
    shifts = lax.broadcasted_iota(jnp.int32, spread.shape, 1)
    flags = jnp.bitwise_and(jnp.right_shift(spread, shifts), 1)
    return flags.reshape(HEAD, tokens).astype(f32).astype(bf16)


def copy_to(src, dst, send, recv, device):
    return pltpu.make_async_remote_copy(
        src_ref=src, dst_ref=dst, send_sem=send, recv_sem=recv,
        device_id=device, device_id_type=MESH,
    )


def kernel(n, heads, tokens, columns, slots, names, pattern, *refs):
    r = types.SimpleNamespace(**dict(zip(names, refs)))
    me = lax.axis_index("ctx")
    dp = lax.axis_index("dp")
    nz, ny = n // 2, 4
    z, y_hi = lax.rem(me, nz), me // nz
    y = 2 * y_hi + dp
    turned = jnp.where(y_hi == 1, z, nz - 1 - z)
    middle = nz // 2 - 1
    chunks = heads * HEAD // CHUNK
    per_head = HEAD // CHUNK
    half = BLK // 2

    def at_ctx(k):
        return {"ctx": k}

    def at_z(k):
        return {"ctx": y_hi * nz + lax.rem(z + k + nz, nz)}

    def at_y(k):
        other = lax.rem(y + k + ny, ny)
        return {"dp": lax.rem(other, 2), "ctx": (other // 2) * nz + z}

    barrier = pltpu.get_barrier_semaphore()

    def greet(i, _):
        pl.semaphore_signal(
            barrier, inc=1, device_id=at_ctx(lax.rem(me + i, n)), device_id_type=MESH
        )
        return 0

    lax.fori_loop(1, n, greet, 0)
    for k in (1, 3):
        pl.semaphore_signal(barrier, inc=1, device_id=at_y(k), device_id_type=MESH)

    loads = {}
    for i, name in enumerate(("gate", "kw", "qw", "v", "do", "xw", "qs", "ks")):
        loads[name] = pltpu.make_async_copy(
            getattr(r, name + "_h"), getattr(r, name), r.in_sem.at[i]
        )
        loads[name].start()

    rows = lax.broadcasted_iota(jnp.int32, (tokens, tokens), 0)
    cols = lax.broadcasted_iota(jnp.int32, (tokens, tokens), 1)
    lower = jnp.where(rows >= cols, 1.0, 0.0)
    lower_bits = lower.astype(bf16)
    loads["gate"].wait()
    gates = r.gate[...]
    r.send1[heads : 2 * heads, :] = jnp.exp(
        jnp.broadcast_to(jnp.sum(gates, axis=1, keepdims=True), (heads, HEAD))
    )
    r.run_rows[...] = lax.dot_general(
        gates, lower, (((1,), (1,)), ((), ())),
        precision=lax.Precision.HIGHEST, preferred_element_type=f32,
    )
    loads["kw"].wait()

    def head_cols(h):
        return pl.ds(pl.multiple_of(h * HEAD, HEAD), HEAD)

    def head_words(h):
        return pl.ds(pl.multiple_of(h * (HEAD // 16), HEAD // 16), HEAD // 16)

    def sums(h, _):
        keys = bits_of(r.kw[head_words(h), :], tokens)
        r.kc[h] = keys
        key_rows = keys.T
        r.kr[h] = key_rows
        spread = jnp.broadcast_to(r.gate[pl.ds(h, 1), :], (HEAD, tokens))
        run = sum(mm_nt(lower_bits, part) for part in split3(spread))
        r.lead[h] = run
        last = jnp.broadcast_to(run[tokens - 1 : tokens, :], (tokens, HEAD))
        end = jnp.exp(last - run)
        r.tail[h] = end
        r.send1[pl.ds(h, 1), :] = jnp.sum(key_rows.astype(f32) * end, axis=0, keepdims=True)
        return 0

    lax.fori_loop(0, heads, sums, 0)
    r.ag1[me] = r.send1[...]
    pl.semaphore_wait(barrier, n + 1)

    def gather(send, target, send_sem, recv_sem, i):
        peer = lax.rem(me + i, n)
        return copy_to(send, target.at[me], send_sem.at[i], recv_sem.at[me], at_ctx(peer))

    def arrival(send, target, send_sem, recv_sem, i):
        peer = lax.rem(me + i, n)
        return copy_to(send, target.at[peer], send_sem.at[i], recv_sem.at[peer], at_ctx(peer))

    def start_gather(*which):
        def one(i, _):
            gather(*which, i).start()
            return 0

        lax.fori_loop(1, n, one, 0)

    def end_gather(*which):
        def one(i, _):
            arrival(*which, i).wait_recv()
            return 0

        lax.fori_loop(1, n, one, 0)

    def sent_gather(*which):
        def one(i, _):
            gather(*which, i).wait_send()
            return 0

        lax.fori_loop(1, n, one, 0)

    first_gather = (r.send1, r.ag1, r.s1_send, r.s1_recv)
    second_gather = (r.gf, r.ag2, r.s2_send, r.s2_recv)
    start_gather(*first_gather)
    loads["qw"].wait()
    loads["v"].wait()

    def local_part(h, _):
        r.qr[h] = bits_of(r.qw[head_words(h), :], tokens).T
        run = r.lead[h]
        run_wide = jnp.concatenate([run, run], axis=1)
        spread = run_wide - jnp.broadcast_to(r.run_rows[pl.ds(h, 1), :], (tokens, tokens))
        mask = jnp.where(rows >= cols, jnp.exp(jnp.minimum(spread, 0.0)), 0.0)
        r.decay[h] = mask
        weights = mm(r.qr[h], r.kc[h]) * mask
        low = weights.astype(bf16)
        r.wl[h] = low
        vh = r.v[:, head_cols(h)]
        r.num[h] = mm(low, vh)
        r.rden[h] = jnp.broadcast_to(jnp.sum(weights, axis=1, keepdims=True), (tokens, HEAD))
        r.yy[h] = mm_exact_left(r.kc[h], r.tail[h] * vh.astype(f32))
        r.lead[h] = jnp.exp(run)
        return 0

    lax.fori_loop(0, heads, local_part, 0)
    end_gather(*first_gather)

    def carry_keys(i, state):
        keys, down, up = state
        item = r.ag1[i]
        factor = item[heads : 2 * heads, :]
        keys = jnp.where(i < me, factor * keys + item[0:heads, :], keys)
        down = jnp.where(jnp.logical_and(i > me, i < nz), down * factor, down)
        up = jnp.where(jnp.logical_and(i < me, i >= nz), up * factor, up)
        return keys, down, up

    ones = jnp.ones((heads, HEAD), f32)
    keys, down, up = lax.fori_loop(0, n, carry_keys, (jnp.zeros((heads, HEAD), f32), ones, ones))
    r.keys_in[...] = keys
    r.mix[...] = down * up
    r.down[...] = jnp.where(y_hi == 0, down, 0.0)
    r.up[...] = jnp.where(y_hi == 1, up, 0.0)
    loads["do"].wait()

    def scaled_part(h, _):
        keys_in = jnp.broadcast_to(r.keys_in[pl.ds(h, 1), :], (HEAD, HEAD))
        high, low = split(keys_in)
        q_rows = r.qr[h]
        met = mm_nt(q_rows, high) + mm_nt(q_rows, low)
        inverse = 1.0 / (1.0 + r.rden[h] + r.lead[h] * met)
        r.rden[h] = inverse
        scaled = r.do[:, head_cols(h)].astype(f32) * inverse
        r.gl[h] = scaled.astype(bf16)
        high, low = split(r.lead[h] * scaled)
        r.xx[h] = mm_tn(q_rows, high) + mm_tn(q_rows, low)
        return 0

    lax.fori_loop(0, heads, scaled_part, 0)
    loads["xw"].wait()

    @pl.when(z == 0)
    def _():
        r.s_in[...] = jnp.zeros_like(r.s_in)

    @pl.when(turned == 0)
    def _():
        r.u_in[...] = jnp.zeros_like(r.u_in)

    @pl.when(z == nz - 1)
    def _():
        r.c_in[...] = jnp.zeros_like(r.c_in)

    def piece(ref, c):
        start = pl.multiple_of(lax.rem(c, per_head) * CHUNK, CHUNK)
        return ref.at[c // per_head, pl.ds(start, CHUNK), :]

    def entry(line, group):
        near = jnp.where(line == 1, nz // 2, nz // 2 - 1)
        return jnp.where(group == 0, near, nz - 1 - near)

    def line_copy(forward, c):
        out, landing, send, recv, step = (
            (r.s_out, r.s_in, r.f_send, r.f_recv, 1)
            if forward
            else (r.c_out, r.c_in, r.b_send, r.b_recv, -1)
        )
        return copy_to(piece(out, c), piece(landing, c), send.at[c], recv.at[c], at_z(step))

    def cross_copy(forward, c):
        line = 1 if forward else 0
        at = line * nz + entry(line, c // (chunks // 2))
        return copy_to(
            piece(r.u_out, c), piece(r.total, c), r.u_send.at[c], r.t_recv.at[c], at_ctx(at)
        )

    def early_copy(c):
        step = jnp.where(y_hi == 1, 1, -1)
        return copy_to(
            piece(r.u_out, c), piece(r.u_in, c), r.u_send.at[c], r.u_recv.at[c], at_z(step)
        )

    def join(c, ref):
        factor = r.mix[pl.ds(c // per_head, 1), :]
        piece(r.u_out, c)[...] = piece(r.u_in, c)[...] + factor * piece(ref, c)[...]

    def pass_early(c):
        @pl.when(turned > 0)
        def _():
            early_copy(c).wait_recv()

        @pl.when(y_hi == 1)
        def _():
            join(c, r.xx)

        @pl.when(y_hi == 0)
        def _():
            join(c, r.yy)

        early_copy(c).start()

    def pass_line(forward, c):
        last = (nz - 1) if forward else 0
        has_in = z > 0 if forward else z < nz - 1
        onward = z != last
        crossing = jnp.logical_and(turned == middle, y_hi == (0 if forward else 1))
        landing, out, add = (r.s_in, r.s_out, r.yy) if forward else (r.c_in, r.c_out, r.xx)

        @pl.when(has_in)
        def _():
            line_copy(forward, c).wait_recv()

        @pl.when(onward)
        def _():
            factor = r.send1[pl.ds(heads + c // per_head, 1), :]
            piece(out, c)[...] = piece(landing, c)[...] * factor + piece(add, c)[...]

            line_copy(forward, c).start()

        @pl.when(crossing)
        def _():
            early_copy(c).wait_recv()
            join(c, out)
            cross_copy(forward, c).start()

    def total_copy(c, step):
        send = r.t_send_down if step < 0 else r.t_send_up
        return copy_to(piece(r.total, c), piece(r.total, c), send.at[c], r.t_recv.at[c], at_z(step))

    def distances(group):
        e = entry(y_hi, group)
        return lax.rem(e - z + nz, nz), lax.rem(z - e + nz, nz)

    def pass_total(group, c):
        below, above = distances(group)
        total_copy(c, -1).wait_recv()

        @pl.when(below < nz // 2)
        def _():
            total_copy(c, -1).start()

        @pl.when(above < nz // 2 - 1)
        def _():
            total_copy(c, 1).start()

    step_words = r.xw.shape[0] // heads

    def side_part(h):
        r.dvl[h] = mm_tn(r.wl[h], r.gl[h])
        at = pl.multiple_of(h * step_words, step_words)
        spread = jnp.broadcast_to(
            r.xw[pl.ds(at, step_words), :][:, None, :], (step_words, 8, tokens)
        )
        shifts = 2 * lax.broadcasted_iota(jnp.int32, spread.shape, 1)
        even = jnp.bitwise_and(jnp.right_shift(spread, shifts), 1)
        odd = jnp.bitwise_and(jnp.right_shift(spread, shifts + 1), 1)
        count = step_words * 8 // half
        to = pl.ds(h * count, count)
        r.xu[to, :, 0:tokens] = even.reshape(count, half, tokens).astype(f32).astype(bf16)
        r.xu[to, :, tokens : 2 * tokens] = odd.reshape(count, half, tokens).astype(f32).astype(bf16)

    f_off = z * HOP
    b_off = (nz - 1 - z) * HOP
    t_off = []
    for group in range(2):
        below, above = distances(group)
        t_off.append(
            nz // 2 * HOP + CROSS + jnp.minimum(below, above) * HOP + group * (chunks // 2)
        )
    u_off = turned * HOP
    side_off = jnp.where(
        z >= nz - 2,
        chunks + 1 + (nz - 1 - z) * HOP,
        jnp.where(jnp.logical_and(y_hi == 1, z <= 1), chunks + 2 + z * (HOP // 2), 0),
    )
    steps = nz * HOP + CROSS + chunks

    def turn(s, _):
        for group in range(2):
            ct = s - t_off[group]

            @pl.when(jnp.logical_and(ct >= 0, ct < chunks // 2))
            def _():
                pass_total(group, ct + group * (chunks // 2))

        cb = s - b_off

        @pl.when(jnp.logical_and(cb >= 0, cb < chunks))
        def _():
            pass_line(False, cb)

        cu = s - u_off

        @pl.when(jnp.logical_and(turned < middle, jnp.logical_and(cu >= 0, cu < chunks)))
        def _():
            pass_early(cu)

        cf = s - f_off

        @pl.when(jnp.logical_and(cf >= 0, cf < chunks))
        def _():
            pass_line(True, cf)

        cs = s - side_off

        @pl.when(jnp.logical_and(cs >= 0, cs < heads))
        def _():
            side_part(cs)

        return 0

    lax.fori_loop(0, steps, turn, 0)

    def product_part(h, _):
        adjoint = r.c_in[h] + r.down[pl.ds(h, 1), :] * r.total[h]
        r.c_in[h] = adjoint
        high, low = split(adjoint)
        k_rows = r.kr[h]
        value = r.dvl[h] + r.tail[h] * (mm(k_rows, high) + mm(k_rows, low))
        pair = value.astype(bf16).astype(f32)
        turned = pltpu.roll(pair, BLK, axis=1)
        left = lax.broadcasted_iota(jnp.int32, pair.shape, 1) < BLK
        zero = jnp.zeros_like(pair)
        for k in range(2):
            upper, under = (pair, turned) if k == 0 else (turned, pair)
            r.rhs[0:tokens, :] = jnp.where(left, upper, zero).astype(bf16)
            r.rhs[tokens : 2 * tokens, :] = jnp.where(left, zero, under).astype(bf16)
            j = 2 * h + k
            for s in range(slots):
                r.lhs[s * half : (s + 1) * half, :] = r.xu[pattern[j, s]]
            result = mm(r.lhs[...], r.rhs[...])
            for s in range(slots):
                r.part[s, j] = result[s * half : (s + 1) * half, :]
        return 0

    def carried_part(h):
        q_rows, k_rows = r.qr[h], r.kr[h]
        high, low = split(r.s_in[h] + r.up[pl.ds(h, 1), :] * r.total[h])
        carried = mm(q_rows, high) + mm(q_rows, low)
        inverse = r.rden[h]
        begin = r.lead[h]
        output = (r.num[h] + begin * carried) * inverse
        given = r.do[:, head_cols(h)].astype(f32)
        slant = -jnp.sum(given * output, axis=1, keepdims=True)
        slant = jnp.broadcast_to(slant, (tokens, HEAD)) * inverse
        scaled = r.gl[h]
        vh = r.v[:, head_cols(h)]
        mixed = mm_nt(scaled, vh) + jnp.concatenate([slant, slant], axis=1)
        mixed = (mixed * r.decay[h]).astype(bf16)
        keys_in = jnp.broadcast_to(r.keys_in[pl.ds(h, 1), :], (tokens, HEAD))
        from_state = mm_nt(scaled, high) + slant * keys_in
        query = mm(mixed, k_rows) + begin * from_state
        r.dq[:, head_cols(h)] = (r.qs[:, head_cols(h)].astype(f32) * query).astype(bf16)
        r.gf[pl.ds(h, 1), :] = jnp.sum(q_rows.astype(f32) * (begin * slant), axis=0, keepdims=True)
        high, low = split(r.c_in[h])
        r.num[h] = mm_tn(mixed, q_rows) + r.tail[h] * (mm_nt(vh, high) + mm_nt(vh, low))

    def second_start():
        r.ag2[me] = r.gf[...]
        start_gather(*second_gather)

    def keys_end():
        end_gather(*second_gather)

        def carry_back(i, state):
            at = n - 1 - i
            new = r.ag2[at] + r.ag1[at][heads : 2 * heads, :] * state
            return jnp.where(at > me, new, state)

        r.keys_in[...] = lax.fori_loop(0, n, carry_back, jnp.zeros((heads, HEAD), f32))

        def keys_part(h, _):
            vector = jnp.broadcast_to(r.keys_in[pl.ds(h, 1), :], (tokens, HEAD))
            key = r.num[h] + r.tail[h] * vector
            r.dk[:, head_cols(h)] = (r.ks[:, head_cols(h)].astype(f32) * key).astype(bf16)
            return 0

        lax.fori_loop(0, heads, keys_part, 0)

    part, zbuf, ybuf = r.part, r.zbuf, r.ybuf
    first, quarter = columns // 2, columns // 4
    zsub = ysub = 4
    zc = first // zsub

    def z_slot(direction, k):
        if direction == 0:
            return lax.rem(z - 1 - k + 2 * nz, nz)
        return nz + lax.rem(z + 1 + k, nz)

    def z_copy(direction, k, c):
        if k == 0:
            src = part.at[z_slot(direction, 0), pl.ds(c * zc, zc)]
        else:
            src = zbuf.at[direction, k - 1, pl.ds(c * zc, zc)]
        return copy_to(
            src, zbuf.at[direction, k, pl.ds(c * zc, zc)],
            r.zs.at[direction, k, c], r.zr.at[direction, k, c],
            at_z(1 if direction == 0 else -1),
        )

    def z_take(direction, k, c):
        z_copy(direction, k, c).wait_recv()
        where = (direction, k, pl.ds(c * zc, zc))
        zbuf[where] = zbuf[where] + part[z_slot(direction, k + 1), pl.ds(c * zc, zc)]

    def y_place(direction, k, c):
        step = -1 - k if direction == 0 else 1 + k
        to = lax.rem(y + step + 2 * ny, ny)
        slot = (to // 2) * nz + direction * (nz // 2) + c
        return slot, pl.multiple_of(first + quarter * lax.rem(to, 2), quarter)

    def y_copy(direction, k, c):
        if k == 0:
            slot, col = y_place(direction, 0, c)
            src = part.at[slot, pl.ds(col, quarter)]
        else:
            src = ybuf.at[k - 1, direction * (nz // 2) + c]
        return copy_to(
            src, ybuf.at[k, direction * (nz // 2) + c],
            r.ys.at[direction, k, c], r.yr.at[direction, k, c],
            at_y(1 if direction == 0 else -1),
        )

    def y_take(direction, k, c):
        y_copy(direction, k, c).wait_recv()
        slot, col = y_place(direction, k + 1, c)
        where = (k, direction * (nz // 2) + c)
        ybuf[where] = ybuf[where] + part[slot, pl.ds(col, quarter)]

    lax.fori_loop(0, heads // 2, product_part, 0)
    for c in range(zsub):
        for direction in (0, 1):
            z_copy(direction, 0, c).start()
    lax.fori_loop(heads // 2, heads, product_part, 0)
    for c in range(ysub):
        for direction in (0, 1):
            y_copy(direction, 0, c).start()
    loads["qs"].wait()
    loads["ks"].wait()

    events = []
    for k in range(nz - 1):
        for c in range(zsub):
            events.append((k + c / zsub, 0, k, c))
    for k in range(ny - 1):
        for c in range(ysub):
            events.append((2 * k + 2 * c / ysub + 0.9, 1, k, c))
    for h in range(heads):
        events.append((0.3 + 4.0 * h / heads, 2, h, 0))
    events.append((4.3, 3, 0, 0))
    events.sort()
    for _, kind, k, c in events:
        if kind == 2:
            carried_part(k)
            continue
        if kind == 3:
            second_start()
            continue
        for direction in (0, 1):
            if kind == 0:
                z_take(direction, k, c)
                if k < nz - 2:
                    z_copy(direction, k + 1, c).start()
            else:
                y_take(direction, k, c)
                if k < ny - 2:
                    y_copy(direction, k + 1, c).start()

    def a_copy(k):
        to = lax.rem(y + k, ny)
        col = pl.multiple_of(quarter * lax.rem(to, 2), quarter)
        return copy_to(
            zbuf.at[to // 2, nz - 2, pl.ds(col, quarter)], r.abuf.at[k],
            r.as_.at[k], r.ar.at[k], at_y(k),
        )

    def b_copy(k):
        return copy_to(
            ybuf.at[ny - 2, lax.rem(z + k, nz)], r.bbuf.at[k], r.bs.at[k], r.br.at[k], at_z(k)
        )

    a_copies = [a_copy(k) for k in range(1, ny)]
    b_copies = [b_copy(k) for k in range(1, nz)]
    for c in b_copies + a_copies:
        c.start()
    keys_end()
    mine, theirs = r.mine, r.theirs
    col = pl.multiple_of(quarter * dp, quarter)
    mine[0] = zbuf[y_hi, nz - 2, pl.ds(col, quarter)]
    mine[1] = ybuf[ny - 2, z]
    for k, c in enumerate(a_copies):
        c.wait_recv()
        mine[0] = mine[0] + r.abuf[k + 1]
    for k, c in enumerate(b_copies):
        c.wait_recv()
        mine[1] = mine[1] + r.bbuf[k + 1]
    swap = copy_to(mine, theirs, r.es.at[0], r.er.at[0], {"dp": 1 - dp})
    swap.start()
    swap.wait_recv()

    for k in range(2):
        own, other = mine[k], theirs[k]
        low, high = 2 * k * quarter, (2 * k + 1) * quarter
        r.blocks[low : low + quarter] = jnp.where(dp == 0, own, other)
        r.blocks[high : high + quarter] = jnp.where(dp == 0, other, own)
    for k in range(half):
        r.out[:, k * HEAD : (k + 1) * HEAD] = r.blocks[:, k, :]

    swap.wait_send()
    for c in a_copies + b_copies:
        c.wait_send()
    for direction in (0, 1):
        for k in range(nz - 1):
            for c in range(zsub):
                z_copy(direction, k, c).wait_send()
        for k in range(ny - 1):
            for c in range(ysub):
                y_copy(direction, k, c).wait_send()
    sent_gather(*first_gather)
    sent_gather(*second_gather)

    @pl.when(turned <= middle)
    def _():
        def one(c, _):
            early_copy(c).wait_send()
            return 0

        lax.fori_loop(0, chunks, one, 0)

    @pl.when(z < nz - 1)
    def _():
        def one(c, _):
            line_copy(True, c).wait_send()
            return 0

        lax.fori_loop(0, chunks, one, 0)

    @pl.when(z > 0)
    def _():
        def one(c, _):
            line_copy(False, c).wait_send()
            return 0

        lax.fori_loop(0, chunks, one, 0)

    for group in range(2):
        below, above = distances(group)
        span = (group * (chunks // 2), (group + 1) * (chunks // 2))

        @pl.when(below < nz // 2)
        def _():
            def one(c, _):
                total_copy(c, -1).wait_send()
                return 0

            lax.fori_loop(*span, one, 0)

        @pl.when(above < nz // 2 - 1)
        def _():
            def one(c, _):
                total_copy(c, 1).wait_send()
                return 0

            lax.fori_loop(*span, one, 0)


def per_device(xw, qw, kw, v, qs, ks, do, gate, pattern):
    tokens, width = v.shape
    heads = width // HEAD
    words = xw.shape[0]
    columns, slots = pattern.shape
    n = lax.axis_size("ctx")
    nz, ny = n // 2, 4
    chunks = heads * HEAD // CHUNK
    half = BLK // 2
    flat = jax.ShapeDtypeStruct((tokens, width), bf16)
    vmem, dma = pltpu.VMEM, pltpu.SemaphoreType.DMA
    scratch = dict(
        gate=vmem(gate.shape, f32),
        kw=vmem(kw.shape, jnp.int32),
        qw=vmem(qw.shape, jnp.int32),
        v=vmem(v.shape, bf16),
        do=vmem(v.shape, bf16),
        xw=vmem(xw.shape, jnp.int32),
        qs=vmem(v.shape, bf16),
        ks=vmem(v.shape, bf16),
        in_sem=dma((8,)),
        kc=vmem((heads, HEAD, tokens), bf16),
        kr=vmem((heads, tokens, HEAD), bf16),
        qr=vmem((heads, tokens, HEAD), bf16),
        gl=vmem((heads, tokens, HEAD), bf16),
        wl=vmem((heads, tokens, tokens), bf16),
        decay=vmem((heads, tokens, tokens), f32),
        xu=vmem((words * 8 // half, half, 2 * tokens), bf16),
        lhs=vmem((slots * half, 2 * tokens), bf16),
        rhs=vmem((2 * tokens, HEAD), bf16),
        part=vmem((slots, columns, half, HEAD), f32),
        send1=vmem((2 * heads, HEAD), f32),
        ag1=vmem((n, 2 * heads, HEAD), f32),
        ag2=vmem((n, heads, HEAD), f32),
        zbuf=vmem((2, nz - 1, columns // 2, half, HEAD), f32),
        ybuf=vmem((ny - 1, nz, columns // 4, half, HEAD), f32),
        abuf=vmem((ny, columns // 4, half, HEAD), f32),
        bbuf=vmem((nz, columns // 4, half, HEAD), f32),
        mine=vmem((2, columns // 4, half, HEAD), f32),
        theirs=vmem((2, columns // 4, half, HEAD), f32),
        blocks=vmem((columns, half, HEAD), f32),
        run_rows=vmem((heads, tokens), f32),
        zs=dma((2, nz - 1, 4)),
        zr=dma((2, nz - 1, 4)),
        ys=dma((2, ny - 1, 4)),
        yr=dma((2, ny - 1, 4)),
        as_=dma((ny,)),
        ar=dma((ny,)),
        bs=dma((nz,)),
        br=dma((nz,)),
        es=dma((1,)),
        er=dma((1,)),
    )
    for name in ("lead", "tail", "num", "rden", "dvl"):
        scratch[name] = vmem((heads, tokens, HEAD), f32)
    for name in ("yy", "s_in", "s_out", "xx", "c_in", "c_out", "total", "u_in", "u_out"):
        scratch[name] = vmem((heads, HEAD, HEAD), f32)
    for name in ("gf", "keys_in", "down", "up", "mix"):
        scratch[name] = vmem((heads, HEAD), f32)
    for name in ("s1_send", "s1_recv", "s2_send", "s2_recv"):
        scratch[name] = dma((n,))
    for name in ("f_send", "f_recv", "b_send", "b_recv", "t_recv", "t_send_up", "t_send_down", "u_send", "u_recv"):
        scratch[name] = dma((chunks,))
    arguments = ("xw_h", "qw_h", "kw_h", "v_h", "do_h", "gate_h", "qs_h", "ks_h")
    names = arguments + ("dq", "dk", "out") + tuple(scratch)
    whole = pl.BlockSpec(memory_space=pltpu.VMEM)
    dq, dk, out = pl.pallas_call(
        functools.partial(kernel, n, heads, tokens, columns, slots, names),
        out_shape=(flat, flat, jax.ShapeDtypeStruct((columns, BLK * BLK), f32)),
        in_specs=[pl.BlockSpec(memory_space=pltpu.SMEM)] + [pl.BlockSpec(memory_space=pl.ANY)] * 8,
        out_specs=(whole, whole, whole),
        scratch_shapes=list(scratch.values()),
        compiler_params=pltpu.CompilerParams(
            collective_id=0, has_side_effects=True, vmem_limit_bytes=60 << 20
        ),
        name="layer",
    )(pattern, xw, qw, kw, v, do, gate, qs, ks)
    return dq, dk, out.reshape(1, columns, BLK * BLK)


def solution(mesh):
    column = P("tensor", ("dp", "ctx"))
    token = P(("dp", "ctx"), "tensor")
    in_specs = (
        P(None, ("dp", "ctx")), column, column, token, token, token, token, column, P("tensor", None)
    )
    return jax.shard_map(
        per_device,
        mesh=mesh,
        in_specs=in_specs,
        out_specs=(token, token, P("ctx", "tensor", None)),
        check_vma=False,
    )
```

```python
import functools
import types

import jax
import jax.numpy as jnp
from jax import lax
from jax.experimental import pallas as pl
from jax.experimental.pallas import tpu as pltpu
from jax.sharding import PartitionSpec as P

HEAD = 128
BLK = 64
SEL = 16
MESH = pl.DeviceIdType.MESH
CHUNK = 32
HOP = 8
CROSS = 28
f32 = jnp.float32
bf16 = jnp.bfloat16


def mm(a, b):
    return lax.dot_general(a, b, (((1,), (0,)), ((), ())), preferred_element_type=f32)


def mm_nt(a, b):
    return lax.dot_general(a, b, (((1,), (1,)), ((), ())), preferred_element_type=f32)


def mm_tn(a, b):
    return lax.dot_general(a, b, (((0,), (0,)), ((), ())), preferred_element_type=f32)


def split(a):
    high = a.astype(bf16)
    return high, (a - high.astype(f32)).astype(bf16)


def split3(a):
    high = a.astype(bf16)
    rest = a - high.astype(f32)
    return (high, *split(rest))


def mm_exact_left(a, b):
    high, low = split(b)
    return mm(a, high) + mm(a, low)


def bits_of(words, tokens):
    spread = jnp.broadcast_to(words[:, None, :], (HEAD // 16, 16, tokens))
    shifts = lax.broadcasted_iota(jnp.int32, spread.shape, 1)
    flags = jnp.bitwise_and(jnp.right_shift(spread, shifts), 1)
    return flags.reshape(HEAD, tokens).astype(f32).astype(bf16)


def copy_to(src, dst, send, recv, device):
    return pltpu.make_async_remote_copy(
        src_ref=src, dst_ref=dst, send_sem=send, recv_sem=recv,
        device_id=device, device_id_type=MESH,
    )


def kernel(n, heads, tokens, columns, slots, names, pattern, *refs):
    r = types.SimpleNamespace(**dict(zip(names, refs)))
    me = lax.axis_index("ctx")
    dp = lax.axis_index("dp")
    nz, ny = n // 2, 4
    z, y_hi = lax.rem(me, nz), me // nz
    y = 2 * y_hi + dp
    turned = jnp.where(y_hi == 1, z, nz - 1 - z)
    middle = nz // 2 - 1
    chunks = heads * HEAD // CHUNK
    per_head = HEAD // CHUNK
    half = BLK // 2

    def at_ctx(k):
        return {"ctx": k}

    def at_z(k):
        return {"ctx": y_hi * nz + lax.rem(z + k + nz, nz)}

    def at_y(k):
        other = lax.rem(y + k + ny, ny)
        return {"dp": lax.rem(other, 2), "ctx": (other // 2) * nz + z}

    barrier = pltpu.get_barrier_semaphore()

    def greet(i, _):
        pl.semaphore_signal(
            barrier, inc=1, device_id=at_ctx(lax.rem(me + i, n)), device_id_type=MESH
        )
        return 0

    lax.fori_loop(1, n, greet, 0)
    for k in (1, 3):
        pl.semaphore_signal(barrier, inc=1, device_id=at_y(k), device_id_type=MESH)

    loads = {}
    for i, name in enumerate(("gate", "kw", "qw", "v", "do", "xw", "qs", "ks")):
        loads[name] = pltpu.make_async_copy(
            getattr(r, name + "_h"), getattr(r, name), r.in_sem.at[i]
        )
        loads[name].start()

    rows = lax.broadcasted_iota(jnp.int32, (tokens, tokens), 0)
    cols = lax.broadcasted_iota(jnp.int32, (tokens, tokens), 1)
    lower = jnp.where(rows >= cols, 1.0, 0.0)
    lower_bits = lower.astype(bf16)
    loads["gate"].wait()
    gates = r.gate[...]
    r.send1[heads : 2 * heads, :] = jnp.exp(
        jnp.broadcast_to(jnp.sum(gates, axis=1, keepdims=True), (heads, HEAD))
    )
    r.run_rows[...] = lax.dot_general(
        gates, lower, (((1,), (1,)), ((), ())),
        precision=lax.Precision.HIGHEST, preferred_element_type=f32,
    )
    loads["kw"].wait()

    def head_cols(h):
        return pl.ds(pl.multiple_of(h * HEAD, HEAD), HEAD)

    def head_words(h):
        return pl.ds(pl.multiple_of(h * (HEAD // 16), HEAD // 16), HEAD // 16)

    def sums(h, _):
        keys = bits_of(r.kw[head_words(h), :], tokens)
        r.kc[h] = keys
        key_rows = keys.T
        r.kr[h] = key_rows
        spread = jnp.broadcast_to(r.gate[pl.ds(h, 1), :], (HEAD, tokens))
        run = sum(mm_nt(lower_bits, part) for part in split3(spread))
        r.lead[h] = run
        last = jnp.broadcast_to(run[tokens - 1 : tokens, :], (tokens, HEAD))
        end = jnp.exp(last - run)
        r.tail[h] = end
        r.send1[pl.ds(h, 1), :] = jnp.sum(key_rows.astype(f32) * end, axis=0, keepdims=True)
        return 0

    lax.fori_loop(0, heads, sums, 0)
    r.ag1[me] = r.send1[...]
    pl.semaphore_wait(barrier, n + 1)

    def gather(send, target, send_sem, recv_sem, i):
        peer = lax.rem(me + i, n)
        return copy_to(send, target.at[me], send_sem.at[i], recv_sem.at[me], at_ctx(peer))

    def arrival(send, target, send_sem, recv_sem, i):
        peer = lax.rem(me + i, n)
        return copy_to(send, target.at[peer], send_sem.at[i], recv_sem.at[peer], at_ctx(peer))

    def start_gather(*which):
        def one(i, _):
            gather(*which, i).start()
            return 0

        lax.fori_loop(1, n, one, 0)

    def end_gather(*which):
        def one(i, _):
            arrival(*which, i).wait_recv()
            return 0

        lax.fori_loop(1, n, one, 0)

    def sent_gather(*which):
        def one(i, _):
            gather(*which, i).wait_send()
            return 0

        lax.fori_loop(1, n, one, 0)

    first_gather = (r.send1, r.ag1, r.s1_send, r.s1_recv)
    second_gather = (r.gf, r.ag2, r.s2_send, r.s2_recv)
    start_gather(*first_gather)
    loads["qw"].wait()
    loads["v"].wait()

    def local_part(h, _):
        r.qr[h] = bits_of(r.qw[head_words(h), :], tokens).T
        run = r.lead[h]
        run_wide = jnp.concatenate([run, run], axis=1)
        spread = run_wide - jnp.broadcast_to(r.run_rows[pl.ds(h, 1), :], (tokens, tokens))
        mask = jnp.where(rows >= cols, jnp.exp(jnp.minimum(spread, 0.0)), 0.0)
        r.decay[h] = mask
        weights = mm(r.qr[h], r.kc[h]) * mask
        low = weights.astype(bf16)
        r.wl[h] = low
        vh = r.v[:, head_cols(h)]
        r.num[h] = mm(low, vh)
        r.rden[h] = jnp.broadcast_to(jnp.sum(weights, axis=1, keepdims=True), (tokens, HEAD))
        r.yy[h] = mm_exact_left(r.kc[h], r.tail[h] * vh.astype(f32))
        r.lead[h] = jnp.exp(run)
        return 0

    lax.fori_loop(0, heads, local_part, 0)
    end_gather(*first_gather)

    def carry_keys(i, state):
        keys, down, up = state
        item = r.ag1[i]
        factor = item[heads : 2 * heads, :]
        keys = jnp.where(i < me, factor * keys + item[0:heads, :], keys)
        down = jnp.where(jnp.logical_and(i > me, i < nz), down * factor, down)
        up = jnp.where(jnp.logical_and(i < me, i >= nz), up * factor, up)
        return keys, down, up

    ones = jnp.ones((heads, HEAD), f32)
    keys, down, up = lax.fori_loop(0, n, carry_keys, (jnp.zeros((heads, HEAD), f32), ones, ones))
    r.keys_in[...] = keys
    r.mix[...] = down * up
    r.down[...] = jnp.where(y_hi == 0, down, 0.0)
    r.up[...] = jnp.where(y_hi == 1, up, 0.0)
    loads["do"].wait()

    def scaled_part(h, _):
        keys_in = jnp.broadcast_to(r.keys_in[pl.ds(h, 1), :], (HEAD, HEAD))
        high, low = split(keys_in)
        q_rows = r.qr[h]
        met = mm_nt(q_rows, high) + mm_nt(q_rows, low)
        inverse = 1.0 / (1.0 + r.rden[h] + r.lead[h] * met)
        r.rden[h] = inverse
        scaled = r.do[:, head_cols(h)].astype(f32) * inverse
        r.gl[h] = scaled.astype(bf16)
        high, low = split(r.lead[h] * scaled)
        r.xx[h] = mm_tn(q_rows, high) + mm_tn(q_rows, low)
        return 0

    lax.fori_loop(0, heads, scaled_part, 0)
    loads["xw"].wait()

    @pl.when(z == 0)
    def _():
        r.s_in[...] = jnp.zeros_like(r.s_in)

    @pl.when(turned == 0)
    def _():
        r.u_in[...] = jnp.zeros_like(r.u_in)

    @pl.when(z == nz - 1)
    def _():
        r.c_in[...] = jnp.zeros_like(r.c_in)

    def piece(ref, c):
        start = pl.multiple_of(lax.rem(c, per_head) * CHUNK, CHUNK)
        return ref.at[c // per_head, pl.ds(start, CHUNK), :]

    def entry(line, group):
        near = jnp.where(line == 1, nz // 2, nz // 2 - 1)
        return jnp.where(group == 0, near, nz - 1 - near)

    def line_copy(forward, c):
        out, landing, send, recv, step = (
            (r.s_out, r.s_in, r.f_send, r.f_recv, 1)
            if forward
            else (r.c_out, r.c_in, r.b_send, r.b_recv, -1)
        )
        return copy_to(piece(out, c), piece(landing, c), send.at[c], recv.at[c], at_z(step))

    def cross_copy(forward, c):
        line = 1 if forward else 0
        at = line * nz + entry(line, c // (chunks // 2))
        return copy_to(
            piece(r.u_out, c), piece(r.total, c), r.u_send.at[c], r.t_recv.at[c], at_ctx(at)
        )

    def early_copy(c):
        step = jnp.where(y_hi == 1, 1, -1)
        return copy_to(
            piece(r.u_out, c), piece(r.u_in, c), r.u_send.at[c], r.u_recv.at[c], at_z(step)
        )

    def join(c, ref):
        factor = r.mix[pl.ds(c // per_head, 1), :]
        piece(r.u_out, c)[...] = piece(r.u_in, c)[...] + factor * piece(ref, c)[...]

    def pass_early(c):
        @pl.when(turned > 0)
        def _():
            early_copy(c).wait_recv()

        @pl.when(y_hi == 1)
        def _():
            join(c, r.xx)

        @pl.when(y_hi == 0)
        def _():
            join(c, r.yy)

        early_copy(c).start()

    def pass_line(forward, c):
        last = (nz - 1) if forward else 0
        has_in = z > 0 if forward else z < nz - 1
        onward = z != last
        crossing = jnp.logical_and(turned == middle, y_hi == (0 if forward else 1))
        landing, out, add = (r.s_in, r.s_out, r.yy) if forward else (r.c_in, r.c_out, r.xx)

        @pl.when(has_in)
        def _():
            line_copy(forward, c).wait_recv()

        @pl.when(onward)
        def _():
            factor = r.send1[pl.ds(heads + c // per_head, 1), :]
            piece(out, c)[...] = piece(landing, c)[...] * factor + piece(add, c)[...]

            line_copy(forward, c).start()

        @pl.when(crossing)
        def _():
            early_copy(c).wait_recv()
            join(c, out)
            cross_copy(forward, c).start()

    def total_copy(c, step):
        send = r.t_send_down if step < 0 else r.t_send_up
        return copy_to(piece(r.total, c), piece(r.total, c), send.at[c], r.t_recv.at[c], at_z(step))

    def distances(group):
        e = entry(y_hi, group)
        return lax.rem(e - z + nz, nz), lax.rem(z - e + nz, nz)

    def pass_total(group, c):
        below, above = distances(group)
        total_copy(c, -1).wait_recv()

        @pl.when(below < nz // 2)
        def _():
            total_copy(c, -1).start()

        @pl.when(above < nz // 2 - 1)
        def _():
            total_copy(c, 1).start()

    step_words = r.xw.shape[0] // heads

    def side_part(h):
        r.dvl[h] = mm_tn(r.wl[h], r.gl[h])
        at = pl.multiple_of(h * step_words, step_words)
        spread = jnp.broadcast_to(
            r.xw[pl.ds(at, step_words), :][:, None, :], (step_words, 8, tokens)
        )
        shifts = 2 * lax.broadcasted_iota(jnp.int32, spread.shape, 1)
        even = jnp.bitwise_and(jnp.right_shift(spread, shifts), 1)
        odd = jnp.bitwise_and(jnp.right_shift(spread, shifts + 1), 1)
        count = step_words * 8 // half
        to = pl.ds(h * count, count)
        r.xu[to, :, 0:tokens] = even.reshape(count, half, tokens).astype(f32).astype(bf16)
        r.xu[to, :, tokens : 2 * tokens] = odd.reshape(count, half, tokens).astype(f32).astype(bf16)

    f_off = z * HOP
    b_off = (nz - 1 - z) * HOP
    t_off = []
    for group in range(2):
        below, above = distances(group)
        t_off.append(
            nz // 2 * HOP + CROSS + jnp.minimum(below, above) * HOP + group * (chunks // 2)
        )
    u_off = turned * HOP
    side_off = jnp.where(
        z >= nz - 2,
        chunks + 1 + (nz - 1 - z) * HOP,
        jnp.where(jnp.logical_and(y_hi == 1, z <= 1), chunks + 2 + z * (HOP // 2), 0),
    )
    steps = nz * HOP + CROSS + chunks

    def turn(s, _):
        for group in range(2):
            ct = s - t_off[group]

            @pl.when(jnp.logical_and(ct >= 0, ct < chunks // 2))
            def _():
                pass_total(group, ct + group * (chunks // 2))

        cb = s - b_off

        @pl.when(jnp.logical_and(cb >= 0, cb < chunks))
        def _():
            pass_line(False, cb)

        cu = s - u_off

        @pl.when(jnp.logical_and(turned < middle, jnp.logical_and(cu >= 0, cu < chunks)))
        def _():
            pass_early(cu)

        cf = s - f_off

        @pl.when(jnp.logical_and(cf >= 0, cf < chunks))
        def _():
            pass_line(True, cf)

        cs = s - side_off

        @pl.when(jnp.logical_and(cs >= 0, cs < heads))
        def _():
            side_part(cs)

        return 0

    lax.fori_loop(0, steps, turn, 0)

    def product_part(h, _):
        adjoint = r.c_in[h] + r.down[pl.ds(h, 1), :] * r.total[h]
        r.c_in[h] = adjoint
        high, low = split(adjoint)
        k_rows = r.kr[h]
        value = r.dvl[h] + r.tail[h] * (mm(k_rows, high) + mm(k_rows, low))
        pair = value.astype(bf16).astype(f32)
        turned = pltpu.roll(pair, BLK, axis=1)
        left = lax.broadcasted_iota(jnp.int32, pair.shape, 1) < BLK
        zero = jnp.zeros_like(pair)
        for k in range(2):
            upper, under = (pair, turned) if k == 0 else (turned, pair)
            r.rhs[0:tokens, :] = jnp.where(left, upper, zero).astype(bf16)
            r.rhs[tokens : 2 * tokens, :] = jnp.where(left, zero, under).astype(bf16)
            j = 2 * h + k
            for s in range(slots):
                r.lhs[s * half : (s + 1) * half, :] = r.xu[pattern[j, s]]
            result = mm(r.lhs[...], r.rhs[...])
            for s in range(slots):
                r.part[s, j] = result[s * half : (s + 1) * half, :]
        return 0

    def carried_part(h):
        q_rows, k_rows = r.qr[h], r.kr[h]
        high, low = split(r.s_in[h] + r.up[pl.ds(h, 1), :] * r.total[h])
        carried = mm(q_rows, high) + mm(q_rows, low)
        inverse = r.rden[h]
        begin = r.lead[h]
        output = (r.num[h] + begin * carried) * inverse
        given = r.do[:, head_cols(h)].astype(f32)
        slant = -jnp.sum(given * output, axis=1, keepdims=True)
        slant = jnp.broadcast_to(slant, (tokens, HEAD)) * inverse
        scaled = r.gl[h]
        vh = r.v[:, head_cols(h)]
        mixed = mm_nt(scaled, vh) + jnp.concatenate([slant, slant], axis=1)
        mixed = (mixed * r.decay[h]).astype(bf16)
        keys_in = jnp.broadcast_to(r.keys_in[pl.ds(h, 1), :], (tokens, HEAD))
        from_state = mm_nt(scaled, high) + slant * keys_in
        query = mm(mixed, k_rows) + begin * from_state
        r.dq[:, head_cols(h)] = (r.qs[:, head_cols(h)].astype(f32) * query).astype(bf16)
        r.gf[pl.ds(h, 1), :] = jnp.sum(q_rows.astype(f32) * (begin * slant), axis=0, keepdims=True)
        high, low = split(r.c_in[h])
        r.num[h] = mm_tn(mixed, q_rows) + r.tail[h] * (mm_nt(vh, high) + mm_nt(vh, low))

    def second_start():
        r.ag2[me] = r.gf[...]
        start_gather(*second_gather)

    def keys_end():
        end_gather(*second_gather)

        def carry_back(i, state):
            at = n - 1 - i
            new = r.ag2[at] + r.ag1[at][heads : 2 * heads, :] * state
            return jnp.where(at > me, new, state)

        r.keys_in[...] = lax.fori_loop(0, n, carry_back, jnp.zeros((heads, HEAD), f32))

        def keys_part(h, _):
            vector = jnp.broadcast_to(r.keys_in[pl.ds(h, 1), :], (tokens, HEAD))
            key = r.num[h] + r.tail[h] * vector
            r.dk[:, head_cols(h)] = (r.ks[:, head_cols(h)].astype(f32) * key).astype(bf16)
            return 0

        lax.fori_loop(0, heads, keys_part, 0)

    part, zbuf, ybuf = r.part, r.zbuf, r.ybuf
    first, quarter = columns // 2, columns // 4
    zsub = ysub = 4
    zc = first // zsub

    def z_slot(direction, k):
        if direction == 0:
            return lax.rem(z - 1 - k + 2 * nz, nz)
        return nz + lax.rem(z + 1 + k, nz)

    def z_copy(direction, k, c):
        if k == 0:
            src = part.at[z_slot(direction, 0), pl.ds(c * zc, zc)]
        else:
            src = zbuf.at[direction, k - 1, pl.ds(c * zc, zc)]
        return copy_to(
            src, zbuf.at[direction, k, pl.ds(c * zc, zc)],
            r.zs.at[direction, k, c], r.zr.at[direction, k, c],
            at_z(1 if direction == 0 else -1),
        )

    def z_take(direction, k, c):
        z_copy(direction, k, c).wait_recv()
        where = (direction, k, pl.ds(c * zc, zc))
        zbuf[where] = zbuf[where] + part[z_slot(direction, k + 1), pl.ds(c * zc, zc)]

    def y_place(direction, k, c):
        step = -1 - k if direction == 0 else 1 + k
        to = lax.rem(y + step + 2 * ny, ny)
        slot = (to // 2) * nz + direction * (nz // 2) + c
        return slot, pl.multiple_of(first + quarter * lax.rem(to, 2), quarter)

    def y_copy(direction, k, c):
        if k == 0:
            slot, col = y_place(direction, 0, c)
            src = part.at[slot, pl.ds(col, quarter)]
        else:
            src = ybuf.at[k - 1, direction * (nz // 2) + c]
        return copy_to(
            src, ybuf.at[k, direction * (nz // 2) + c],
            r.ys.at[direction, k, c], r.yr.at[direction, k, c],
            at_y(1 if direction == 0 else -1),
        )

    def y_take(direction, k, c):
        y_copy(direction, k, c).wait_recv()
        slot, col = y_place(direction, k + 1, c)
        where = (k, direction * (nz // 2) + c)
        ybuf[where] = ybuf[where] + part[slot, pl.ds(col, quarter)]

    lax.fori_loop(0, heads // 2, product_part, 0)
    for c in range(zsub):
        for direction in (0, 1):
            z_copy(direction, 0, c).start()
    lax.fori_loop(heads // 2, heads, product_part, 0)
    for c in range(ysub):
        for direction in (0, 1):
            y_copy(direction, 0, c).start()
    loads["qs"].wait()
    loads["ks"].wait()

    events = []
    for k in range(nz - 1):
        for c in range(zsub):
            events.append((k + c / zsub, 0, k, c))
    for k in range(ny - 1):
        for c in range(ysub):
            events.append((2 * k + 2 * c / ysub + 0.9, 1, k, c))
    for h in range(heads):
        events.append((0.3 + 4.0 * h / heads, 2, h, 0))
    events.append((4.3, 3, 0, 0))
    events.sort()
    for _, kind, k, c in events:
        if kind == 2:
            carried_part(k)
            continue
        if kind == 3:
            second_start()
            continue
        for direction in (0, 1):
            if kind == 0:
                z_take(direction, k, c)
                if k < nz - 2:
                    z_copy(direction, k + 1, c).start()
            else:
                y_take(direction, k, c)
                if k < ny - 2:
                    y_copy(direction, k + 1, c).start()

    def a_copy(k):
        to = lax.rem(y + k, ny)
        col = pl.multiple_of(quarter * lax.rem(to, 2), quarter)
        return copy_to(
            zbuf.at[to // 2, nz - 2, pl.ds(col, quarter)], r.abuf.at[k],
            r.as_.at[k], r.ar.at[k], at_y(k),
        )

    def b_copy(k):
        return copy_to(
            ybuf.at[ny - 2, lax.rem(z + k, nz)], r.bbuf.at[k], r.bs.at[k], r.br.at[k], at_z(k)
        )

    a_copies = [a_copy(k) for k in range(1, ny)]
    b_copies = [b_copy(k) for k in range(1, nz)]
    for c in b_copies + a_copies:
        c.start()
    keys_end()
    mine, theirs = r.mine, r.theirs
    col = pl.multiple_of(quarter * dp, quarter)
    mine[0] = zbuf[y_hi, nz - 2, pl.ds(col, quarter)]
    mine[1] = ybuf[ny - 2, z]
    for k, c in enumerate(a_copies):
        c.wait_recv()
        mine[0] = mine[0] + r.abuf[k + 1]
    for k, c in enumerate(b_copies):
        c.wait_recv()
        mine[1] = mine[1] + r.bbuf[k + 1]
    swap = copy_to(mine, theirs, r.es.at[0], r.er.at[0], {"dp": 1 - dp})
    swap.start()
    swap.wait_recv()

    for k in range(2):
        own, other = mine[k], theirs[k]
        low, high = 2 * k * quarter, (2 * k + 1) * quarter
        r.blocks[low : low + quarter] = jnp.where(dp == 0, own, other)
        r.blocks[high : high + quarter] = jnp.where(dp == 0, other, own)
    for k in range(half):
        r.out[:, k * HEAD : (k + 1) * HEAD] = r.blocks[:, k, :]

    swap.wait_send()
    for c in a_copies + b_copies:
        c.wait_send()
    for direction in (0, 1):
        for k in range(nz - 1):
            for c in range(zsub):
                z_copy(direction, k, c).wait_send()
        for k in range(ny - 1):
            for c in range(ysub):
                y_copy(direction, k, c).wait_send()
    sent_gather(*first_gather)
    sent_gather(*second_gather)

    @pl.when(turned <= middle)
    def _():
        def one(c, _):
            early_copy(c).wait_send()
            return 0

        lax.fori_loop(0, chunks, one, 0)

    @pl.when(z < nz - 1)
    def _():
        def one(c, _):
            line_copy(True, c).wait_send()
            return 0

        lax.fori_loop(0, chunks, one, 0)

    @pl.when(z > 0)
    def _():
        def one(c, _):
            line_copy(False, c).wait_send()
            return 0

        lax.fori_loop(0, chunks, one, 0)

    for group in range(2):
        below, above = distances(group)
        span = (group * (chunks // 2), (group + 1) * (chunks // 2))

        @pl.when(below < nz // 2)
        def _():
            def one(c, _):
                total_copy(c, -1).wait_send()
                return 0

            lax.fori_loop(*span, one, 0)

        @pl.when(above < nz // 2 - 1)
        def _():
            def one(c, _):
                total_copy(c, 1).wait_send()
                return 0

            lax.fori_loop(*span, one, 0)


def per_device(xw, qw, kw, v, qs, ks, do, gate, pattern):
    tokens, width = v.shape
    heads = width // HEAD
    words = xw.shape[0]
    columns, slots = pattern.shape
    n = lax.axis_size("ctx")
    nz, ny = n // 2, 4
    chunks = heads * HEAD // CHUNK
    half = BLK // 2
    flat = jax.ShapeDtypeStruct((tokens, width), bf16)
    vmem, dma = pltpu.VMEM, pltpu.SemaphoreType.DMA
    scratch = dict(
        gate=vmem(gate.shape, f32),
        kw=vmem(kw.shape, jnp.int32),
        qw=vmem(qw.shape, jnp.int32),
        v=vmem(v.shape, bf16),
        do=vmem(v.shape, bf16),
        xw=vmem(xw.shape, jnp.int32),
        qs=vmem(v.shape, bf16),
        ks=vmem(v.shape, bf16),
        in_sem=dma((8,)),
        kc=vmem((heads, HEAD, tokens), bf16),
        kr=vmem((heads, tokens, HEAD), bf16),
        qr=vmem((heads, tokens, HEAD), bf16),
        gl=vmem((heads, tokens, HEAD), bf16),
        wl=vmem((heads, tokens, tokens), bf16),
        decay=vmem((heads, tokens, tokens), f32),
        xu=vmem((words * 8 // half, half, 2 * tokens), bf16),
        lhs=vmem((slots * half, 2 * tokens), bf16),
        rhs=vmem((2 * tokens, HEAD), bf16),
        part=vmem((slots, columns, half, HEAD), f32),
        send1=vmem((2 * heads, HEAD), f32),
        ag1=vmem((n, 2 * heads, HEAD), f32),
        ag2=vmem((n, heads, HEAD), f32),
        zbuf=vmem((2, nz - 1, columns // 2, half, HEAD), f32),
        ybuf=vmem((ny - 1, nz, columns // 4, half, HEAD), f32),
        abuf=vmem((ny, columns // 4, half, HEAD), f32),
        bbuf=vmem((nz, columns // 4, half, HEAD), f32),
        mine=vmem((2, columns // 4, half, HEAD), f32),
        theirs=vmem((2, columns // 4, half, HEAD), f32),
        blocks=vmem((columns, half, HEAD), f32),
        run_rows=vmem((heads, tokens), f32),
        zs=dma((2, nz - 1, 4)),
        zr=dma((2, nz - 1, 4)),
        ys=dma((2, ny - 1, 4)),
        yr=dma((2, ny - 1, 4)),
        as_=dma((ny,)),
        ar=dma((ny,)),
        bs=dma((nz,)),
        br=dma((nz,)),
        es=dma((1,)),
        er=dma((1,)),
    )
    for name in ("lead", "tail", "num", "rden", "dvl"):
        scratch[name] = vmem((heads, tokens, HEAD), f32)
    for name in ("yy", "s_in", "s_out", "xx", "c_in", "c_out", "total", "u_in", "u_out"):
        scratch[name] = vmem((heads, HEAD, HEAD), f32)
    for name in ("gf", "keys_in", "down", "up", "mix"):
        scratch[name] = vmem((heads, HEAD), f32)
    for name in ("s1_send", "s1_recv", "s2_send", "s2_recv"):
        scratch[name] = dma((n,))
    for name in ("f_send", "f_recv", "b_send", "b_recv", "t_recv", "t_send_up", "t_send_down", "u_send", "u_recv"):
        scratch[name] = dma((chunks,))
    arguments = ("xw_h", "qw_h", "kw_h", "v_h", "do_h", "gate_h", "qs_h", "ks_h")
    names = arguments + ("dq", "dk", "out") + tuple(scratch)
    whole = pl.BlockSpec(memory_space=pltpu.VMEM)
    dq, dk, out = pl.pallas_call(
        functools.partial(kernel, n, heads, tokens, columns, slots, names),
        out_shape=(flat, flat, jax.ShapeDtypeStruct((columns, BLK * BLK), f32)),
        in_specs=[pl.BlockSpec(memory_space=pltpu.SMEM)] + [pl.BlockSpec(memory_space=pl.ANY)] * 8,
        out_specs=(whole, whole, whole),
        scratch_shapes=list(scratch.values()),
        compiler_params=pltpu.CompilerParams(
            collective_id=0, has_side_effects=True, vmem_limit_bytes=60 << 20
        ),
        name="layer",
    )(pattern, xw, qw, kw, v, do, gate, qs, ks)
    return dq, dk, out.reshape(1, columns, BLK * BLK)


def solution(mesh):
    column = P("tensor", ("dp", "ctx"))
    token = P(("dp", "ctx"), "tensor")
    in_specs = (
        P(None, ("dp", "ctx")), column, column, token, token, token, token, column, P("tensor", None)
    )
    return jax.shard_map(
        per_device,
        mesh=mesh,
        in_specs=in_specs,
        out_specs=(token, token, P("ctx", "tensor", None)),
        check_vma=False,
    )
```
